32 devices in a mesh: dp: 8 (over z, y), seq: 4 (over x, core).
Axes of the slice: x: 2, y: 2, z: 4, core: 2. Of those that a mesh axis runs over, the one named last changes fastest.
Arguments:
- tokens: bfloat16 [24, 1040, 1152], P('dp', 'seq'), may hold values from -6 to 6
- skip_tokens: bfloat16 [24, 1040, 1152], P('dp', 'seq'), may hold values from -6 to 6
- skip_weight: bfloat16 [2304, 1152], replicated, may hold values from -0.125 to 0.125
- skip_bias: bfloat16 [1152], replicated, may hold values from -1.75 to 1.75
- attn_norm_gain: bfloat16 [1152], replicated, may hold values from 0.099609375 to 1.8984375
- attn_norm_bias: bfloat16 [1152], replicated, may hold values from -1.75 to 1.75
- qkv_weight: bfloat16 [1152, 3456], replicated, may hold values from -0.25 to 0.25
- proj_weight: bfloat16 [1152, 1152], replicated, may hold values from -0.5 to 0.5
- proj_bias: bfloat16 [1152], replicated, may hold values from -1.75 to 1.75
- ffn_norm_gain: bfloat16 [1152], replicated, may hold values from 0.099609375 to 1.8984375
- ffn_norm_bias: bfloat16 [1152], replicated, may hold values from -1.75 to 1.75
- up_weight: bfloat16 [1152, 4608], replicated, may hold values from -0.1875 to 0.1875
- up_bias: bfloat16 [4608], replicated, may hold values from -1.75 to 1.75
- down_weight: bfloat16 [4608, 1152], replicated, may hold values from -0.09375 to 0.09375
- down_bias: bfloat16 [1152], replicated, may hold values from -1.75 to 1.75
- key_mask: int32 [24, 1040], P('dp'), may hold values from 0 to 1, as said below
- timesteps: int32 [24], P('dp'), may hold values from 0 to 999
- out_grad: bfloat16 [24, 1040, 1152], P('dp', 'seq'), may hold values from -6 to 6
Outputs:
- block_out: bfloat16 [24, 1040, 1152], P('dp', 'seq')
- tokens_grad: bfloat16 [24, 1040, 1152], P('dp', 'seq')
- skip_grad: bfloat16 [24, 1040, 1152], P('dp', 'seq')
- skip_weight_grad: float32 [2304, 1152], P('dp', 'seq')
- qkv_weight_grad: float32 [1152, 3456], P('dp', 'seq')
- proj_weight_grad: float32 [1152, 1152], P('dp', 'seq')
- up_weight_grad: float32 [1152, 4608], P('dp', 'seq')
- down_weight_grad: float32 [4608, 1152], P('dp', 'seq')
- skip_bias_grad: float32 [1152], replicated
- attn_norm_gain_grad: float32 [1152], replicated
- attn_norm_bias_grad: float32 [1152], replicated
- proj_bias_grad: float32 [1152], replicated
- ffn_norm_gain_grad: float32 [1152], replicated
- ffn_norm_bias_grad: float32 [1152], replicated
- up_bias_grad: float32 [4608], replicated
- down_bias_grad: float32 [1152], replicated
The draws below stay inside these ranges and needn't reach their ends.
Inputs may be any that keep to these rules, and one draw needn't show every extreme that they name: `key_mask`: the first token slot of every item is a valid key.
All inputs are finite; a program needn't handle non-finite values.
Results may differ from the reference program's by a relative error of at most 0.02.
Values may be sent and summed in bfloat16 or wider, within the bound.
No kernel may reach another device: no remote copies, remote signals or barrier semaphores. Data moves between devices by JAX's collectives and lax.ppermute only.
A program may use at most 256 MiB of HBM per device.

```python
import math
import jax
import jax.numpy as jnp
from jax import lax

D = 1152
HEADS = 16
FF = 4608
SEQ_LEN = 1040
DIFF_STEPS = 1000
ITEMS = 24


def draw_key_mask(key, part):
    picks = jax.random.randint(key, (ITEMS, SEQ_LEN), 0, 4)
    valid = (picks > 0).astype(jnp.int32)
    return valid.at[:, 0].set(1)


def set_ends(values, rng, low, top_value):
    extent = values.shape
    spot = [jax.random.randint(jax.random.fold_in(rng, axis), (), 0, extent[axis]) for axis in range(len(extent))]
    values = values.at[tuple(spot)].set(low)
    longest = extent.index(max(extent))
    spot[longest] = (spot[longest] + 1) % extent[longest]
    return values.at[tuple(spot)].set(top_value)


def steps_of(rng, extent, cuts, smallest, high):
    def one(dim, shards_of):
        draws = jax.random.uniform(jax.random.fold_in(jax.random.fold_in(rng, 6), dim), (shards_of,), jnp.float32, smallest / len(cuts), high / len(cuts))
        return jnp.repeat(jnp.exp(draws), extent[dim] // shards_of).reshape((-1,) + (1,) * (len(extent) - dim - 1))

    level = one(*cuts[0])
    for cut in cuts[1:]:
        level = level * one(*cut)
    return level


def bell_draw(key, dims, width, reach, shards=(), dtype=jnp.bfloat16):
    loudness = steps_of(key, dims, shards, -0.22, 0.18) if shards else 1.0
    drawn = jax.random.normal(key, dims, jnp.float32) * width * loudness
    return jnp.minimum(jnp.maximum(drawn, -reach), reach).astype(dtype)


def setup_inputs(seed: int = 0) -> dict:
    keys = jax.random.split(jax.random.key(seed), 19)
    tokens = bell_draw(keys[0], (ITEMS, SEQ_LEN, D), 1.0, 6.0, ((0, 8), (1, 4)))
    skip_tokens = bell_draw(keys[1], (ITEMS, SEQ_LEN, D), 1.0, 6.0, ((0, 8), (1, 4)))
    skip_weight = bell_draw(keys[2], (2 * D, D), (2 * D) ** -0.5, 0.125)
    skip_bias = bell_draw(keys[3], (D,), 0.3, 1.75)
    attn_norm_gain = jnp.clip(1.0 + 0.18 * jax.random.normal(keys[4], (D,), jnp.float32), 0.099609375, 1.8984375).astype(jnp.bfloat16)
    attn_norm_bias = bell_draw(keys[5], (D,), 0.3, 1.75)
    qkv_weight = bell_draw(keys[6], (D, 3 * D), (D // 2) ** -0.5, 0.25)
    proj_weight = bell_draw(keys[7], (D, D), (D // 8) ** -0.5, 0.5)
    proj_bias = bell_draw(keys[8], (D,), 0.3, 1.75)
    ffn_norm_gain = jnp.clip(1.0 + 0.18 * jax.random.normal(keys[9], (D,), jnp.float32), 0.099609375, 1.8984375).astype(jnp.bfloat16)
    ffn_norm_bias = bell_draw(keys[10], (D,), 0.3, 1.75)
    up_weight = bell_draw(keys[11], (D, FF), D ** -0.5, 0.1875)
    up_bias = bell_draw(keys[12], (FF,), 0.3, 1.75)
    down_weight = bell_draw(keys[13], (FF, D), FF ** -0.5, 0.09375)
    down_bias = bell_draw(keys[14], (D,), 0.3, 1.75)
    key_mask = draw_key_mask(jax.random.fold_in(keys[18], 71), 0)
    timesteps = set_ends(jax.random.randint(keys[16], (ITEMS,), 0, DIFF_STEPS), jax.random.fold_in(keys[16], 1), 0, DIFF_STEPS - 1).astype(jnp.int32)
    out_grad = bell_draw(keys[17], (ITEMS, SEQ_LEN, D), 1.0, 6.0, ((0, 8), (1, 4)))
    return {"tokens": tokens, "skip_tokens": skip_tokens, "skip_weight": skip_weight, "skip_bias": skip_bias, "attn_norm_gain": attn_norm_gain, "attn_norm_bias": attn_norm_bias, "qkv_weight": qkv_weight, "proj_weight": proj_weight, "proj_bias": proj_bias, "ffn_norm_gain": ffn_norm_gain, "ffn_norm_bias": ffn_norm_bias, "up_weight": up_weight, "up_bias": up_bias, "down_weight": down_weight, "down_bias": down_bias, "key_mask": key_mask, "timesteps": timesteps, "out_grad": out_grad}


EPS = 1e-05

@jax.custom_vjp
def low(v):
    return lax.optimization_barrier(v.astype(jnp.bfloat16)).astype(jnp.float32)

@jax.custom_vjp
def low_back(v):
    return v

def low_keep(v):
    return (low(v), None)

def low_pass(kept, grad):
    return (grad,)

def back_keep(v):
    return (v, None)

def back_low(kept, grad):
    return (low(grad),)
low.defvjp(low_keep, low_pass)
low_back.defvjp(back_keep, back_low)

def matmul(left, right):
    return jnp.dot(left, right, precision=lax.Precision.HIGHEST)

def layer_norm(hidden, gain, shift):
    centered = hidden - lax.optimization_barrier(jnp.mean(hidden, axis=-1, keepdims=True))
    variance = lax.optimization_barrier(jnp.mean(centered * centered, axis=-1, keepdims=True))
    return centered * lax.rsqrt(variance + EPS) * gain + shift

def forward(params, tokens, skip_tokens, key_valid):
    skip_weight, skip_bias, attn_norm_gain, attn_norm_bias, qkv_weight, proj_weight, proj_bias, ffn_norm_gain, ffn_norm_bias, up_weight, up_bias, down_weight, down_bias = params
    token_count = tokens.shape[0]
    head_size = D // HEADS
    merged = low_back(matmul(jnp.concatenate([tokens, skip_tokens], axis=-1), skip_weight) + skip_bias)
    normed = low(layer_norm(merged, attn_norm_gain, attn_norm_bias))
    packed = low_back(low(matmul(normed, qkv_weight))).reshape(token_count, 3, HEADS, head_size)
    queries = packed[:, 0]
    key_rows = packed[:, 1]
    value_rows = packed[:, 2]
    scores = jnp.einsum('qhd,khd->hqk', queries, key_rows, precision=lax.Precision.HIGHEST)
    scores = low_back(scores * head_size ** (-0.5))
    scores = jnp.where(key_valid[None, None, :] > 0, scores, -1e+30)
    row_max = lax.optimization_barrier(jnp.max(scores, axis=-1, keepdims=True))
    expo = jnp.exp(scores - row_max)
    probs = expo / lax.optimization_barrier(jnp.sum(expo, axis=-1, keepdims=True))
    attended = jnp.einsum('hqk,khd->qhd', low(probs), value_rows, precision=lax.Precision.HIGHEST)
    attended = low_back(low(attended)).reshape(token_count, D)
    after_attn = merged + low_back(matmul(attended, proj_weight) + proj_bias)
    normed_ffn = low(layer_norm(after_attn, ffn_norm_gain, ffn_norm_bias))
    pre_act = low_back(matmul(normed_ffn, up_weight) + up_bias)
    activ = low(jax.nn.gelu(pre_act, approximate=False))
    return after_attn + low_back(matmul(activ, down_weight) + down_bias)

def reference(tokens, skip_tokens, skip_weight, skip_bias, attn_norm_gain, attn_norm_bias, qkv_weight, proj_weight, proj_bias, ffn_norm_gain, ffn_norm_bias, up_weight, up_bias, down_weight, down_bias, key_mask, timesteps, out_grad):
    params = tuple((p.astype(jnp.float32) for p in (skip_weight, skip_bias, attn_norm_gain, attn_norm_bias, qkv_weight, proj_weight, proj_bias, ffn_norm_gain, ffn_norm_bias, up_weight, up_bias, down_weight, down_bias)))
    phase = 0.5 * math.pi * timesteps.astype(jnp.float32) / DIFF_STEPS
    loss_weight = 0.5 + jnp.cos(phase) ** 2

    def one_item(carry, item):
        token_rows, skip_rows, valid_row, grad_rows, weight_item = item

        def apply_block(prm, first, second):
            return forward(prm, first, second, valid_row)
        result, pull = jax.vjp(apply_block, params, token_rows.astype(jnp.float32), skip_rows.astype(jnp.float32))
        param_grads, token_back, skip_back = pull(grad_rows.astype(jnp.float32) * weight_item)
        carry = jax.tree.map(lambda acc, new: acc + new, carry, param_grads)
        return (carry, (result.astype(jnp.bfloat16), token_back.astype(jnp.bfloat16), skip_back.astype(jnp.bfloat16)))
    start = tuple((jnp.zeros(p.shape, jnp.float32) for p in params))
    grads, (block_out, tokens_grad, skip_grad) = lax.scan(one_item, start, (tokens, skip_tokens, key_mask, out_grad, loss_weight))
    return (block_out, tokens_grad, skip_grad, grads[0], grads[4], grads[5], grads[9], grads[11], grads[1], grads[2], grads[3], grads[6], grads[7], grads[8], grads[10], grads[12])
```

```python
import functools
import math

import jax
import jax.numpy as jnp
from jax import lax
from jax.experimental import pallas as pl
from jax.experimental.pallas import tpu as pltpu
from jax.sharding import PartitionSpec as P

HEADS = 16
DIFF_STEPS = 1000
EPS = 1e-05
F32 = jnp.float32
BF16 = jnp.bfloat16
VMEM_BYTES = 63 * 1024 * 1024
LOG2E = math.log2(math.e)


def contract_rows(left, right):
    return lax.dot_general(left, right, (((0,), (0,)), ((), ())), preferred_element_type=F32)


def dot(left, right):
    return jnp.dot(left, right, preferred_element_type=F32)


def dot_t(left, right):
    return lax.dot_general(left, right, (((1,), (1,)), ((), ())), preferred_element_type=F32)


def normalize(hidden):
    centered = hidden - jnp.mean(hidden, axis=-1, keepdims=True)
    inverse = lax.rsqrt(jnp.mean(centered * centered, axis=-1, keepdims=True) + EPS)
    return (centered * inverse, inverse)


def norm_back(d_normed, normal_rows, inverse, gain):
    d_plain = d_normed * gain
    d_hidden = inverse * (
        d_plain
        - jnp.mean(d_plain, axis=-1, keepdims=True)
        - normal_rows * jnp.mean(d_plain * normal_rows, axis=-1, keepdims=True)
    )
    gain_sum = jnp.sum(d_normed * normal_rows, axis=0, keepdims=True)
    return (d_hidden, gain_sum, jnp.sum(d_normed, axis=0, keepdims=True))


def whole(shape):
    return pl.BlockSpec(shape, lambda *_: (0,) * len(shape))


def scalars():
    return pl.BlockSpec(memory_space=pltpu.SMEM)


class Out:
    def __init__(self, shape, dtype, spec, prev=None):
        self.shape, self.dtype, self.spec, self.prev = shape, dtype, spec, prev


def call(kernel, name, grid, prefetch, inputs, outs, scratch, flops, moved):
    carried = [(k, out) for k, out in enumerate(outs) if out.prev is not None]
    first_out = len(prefetch) + len(inputs)

    def body(*refs):
        kernel(*refs[:first_out], *refs[first_out + len(carried) :])

    return pl.pallas_call(
        body,
        name=name,
        out_shape=[jax.ShapeDtypeStruct(out.shape, out.dtype) for out in outs],
        grid_spec=pltpu.PrefetchScalarGridSpec(
            num_scalar_prefetch=len(prefetch),
            grid=grid,
            in_specs=[spec for _, spec in inputs] + [pl.BlockSpec(memory_space=pl.ANY)] * len(carried),
            out_specs=[out.spec for out in outs],
            scratch_shapes=scratch,
        ),
        input_output_aliases={first_out + at: k for at, (k, _) in enumerate(carried)},
        compiler_params=pltpu.CompilerParams(vmem_limit_bytes=VMEM_BYTES),
        cost_estimate=pl.CostEstimate(flops=flops, bytes_accessed=moved, transcendentals=0),
    )(*prefetch, *[array for array, _ in inputs], *[out.prev for _, out in carried])


def write_halves(value, half, mine_ref, theirs_ref, core, parts):
    rows, width = value.shape
    block = width // parts
    padded = half.shape[1]
    for parity in range(2):
        for at in range(parts // 2):
            source = (2 * at + parity) * block
            half[parity, :rows, at * block : (at + 1) * block] = value[:, source : source + block]
        if padded > rows:
            half[parity, rows:, :] = jnp.zeros((padded - rows, width // 2), BF16)
    mine_ref[0] = half[core]
    theirs_ref[0] = half[1 - core]


def store_padded(ref, value):
    rows, width = value.shape
    padded = ref.shape[1]
    ref[0, :rows, :] = value
    if padded > rows:
        ref[0, rows:, :] = jnp.zeros((padded - rows, width), BF16)


def front_kernel(parts, seq_ref, tok, skp, skip_w, skip_b, gain, shift, qkv_w, *rest):
    blocks, (merged, normed, cat), (acc, low, packed, groups) = rest[:parts], rest[parts : parts + 3], rest[parts + 3 :]
    step = pl.program_id(0)
    me = seq_ref[0]
    width = acc.shape[1]
    local = width // parts

    @pl.when(step == 0)
    def _():
        acc[...] = dot(tok[0], skip_w[...])
        rows, padded = tok.shape[1], cat.shape[1]
        cat[0, :rows, :width] = tok[0]
        cat[0, :rows, width:] = skp[0]
        if padded > rows:
            cat[0, rows:, :] = jnp.zeros((padded - rows, 2 * width), BF16)

    @pl.when(step == 1)
    def _():
        hidden = acc[...] + dot(skp[0], skip_w[...]) + skip_b[...].astype(F32)
        merged[...] = hidden
        normal, _ = normalize(hidden)
        value = (normal * gain[...].astype(F32) + shift[...].astype(F32)).astype(BF16)
        low[...] = value
        store_padded(normed, value)

    @pl.when(step >= 2)
    def _():
        packed[step - 2] = dot(low[...], qkv_w[...]).astype(BF16)

    @pl.when(step == 4)
    def _():
        for group in range(parts):
            for which in range(3):
                groups[group, :, which * local : (which + 1) * local] = packed[
                    which, :, group * local : (group + 1) * local
                ]
        for k in range(parts):
            blocks[k][...] = groups[me ^ k]


def split_heads(parts, heads, blocks, offset, target):
    seg = blocks[0].shape[0]
    size = target.shape[2]
    for k in range(parts):
        for head in range(heads):
            at = offset + head * size
            target[head, k * seg : (k + 1) * seg, :] = blocks[k][:, at : at + size]


def split_rows(parts, heads, blocks, offset, target):
    size = target.shape[3]
    for k in range(parts):
        for head in range(heads):
            at = offset + head * size
            target[k, head] = blocks[k][:, at : at + size]


def attend_kernel(parts, heads, bias, *rest):
    blocks, outs, (log_sum, queries, keys, values, result) = (
        rest[:parts],
        rest[parts : 2 * parts],
        rest[2 * parts :],
    )
    size = queries.shape[3]
    local = heads * size
    seg = queries.shape[2]
    split_rows(parts, heads, blocks, 0, queries)
    split_heads(parts, heads, blocks, local, keys)
    split_heads(parts, heads, blocks, 2 * local, values)
    scale = size ** (-0.5) * LOG2E
    lane = lax.broadcasted_iota(jnp.int32, (seg, 128), 1)

    @pl.loop(0, parts)
    def _(k):
        sums = jnp.zeros((seg, 128), F32)
        for head in range(heads):
            scores = dot_t(queries[k, head], keys[head]) * scale + bias[0]
            row_max = jnp.max(scores, axis=-1, keepdims=True)
            expo = jnp.exp2(scores - row_max)
            row_sum = jnp.sum(expo, axis=-1, keepdims=True)
            output = dot(expo.astype(BF16), values[head]) / row_sum
            result[k, :, head * size : (head + 1) * size] = output.astype(BF16)
            sums = jnp.where(lane == head, row_max + jnp.log2(row_sum), sums)
        log_sum[k] = sums

    for k in range(parts):
        outs[k][...] = result[k]


def attend_back_kernel(parts, heads, bias, log_sum, *rest):
    blocks, grads, outs = rest[:parts], rest[parts : 2 * parts], rest[2 * parts : 3 * parts]
    queries, keys, values, d_out, d_query, d_key_t, d_value_t, turned = rest[3 * parts :]
    size = queries.shape[3]
    seg = queries.shape[2]
    local = heads * size
    split_rows(parts, heads, blocks, 0, queries)
    split_heads(parts, heads, blocks, local, keys)
    split_heads(parts, heads, blocks, 2 * local, values)
    split_rows(parts, heads, grads, 0, d_out)
    plain = size ** (-0.5)
    scale = plain * LOG2E
    lane = lax.broadcasted_iota(jnp.int32, (seg, 128), 1)
    d_key_t[...] = jnp.zeros_like(d_key_t)
    d_value_t[...] = jnp.zeros_like(d_value_t)

    @pl.loop(0, parts)
    def _(k):
        sums = log_sum[k]
        for head in range(heads):
            query, grad = queries[k, head], d_out[k, head]
            log_row = jnp.sum(jnp.where(lane == head, sums, 0.0), axis=-1, keepdims=True)
            scores = dot_t(query, keys[head]) * scale + bias[0]
            probs = jnp.exp2(scores - log_row)
            d_probs = dot_t(grad, values[head])
            inner = jnp.sum(probs * d_probs, axis=-1, keepdims=True)
            d_scores = (probs * (d_probs - inner)).astype(BF16)
            d_query[k, :, head * size : (head + 1) * size] = (dot(d_scores, keys[head]) * plain).astype(BF16)
            d_key_t[head] += contract_rows(query, d_scores)
            d_value_t[head] += contract_rows(grad, probs.astype(BF16))

    for k in range(parts):
        outs[k][:, :local] = d_query[k]
    for at, source, factor in ((local, d_key_t, plain), (2 * local, d_value_t, 1.0)):
        for head in range(heads):
            turned[...] = jnp.transpose(source[head]) * factor
            for k in range(parts):
                outs[k][:, at + head * size : at + (head + 1) * size] = turned[
                    k * seg : (k + 1) * seg, :
                ].astype(BF16)


def ffn_kernel(parts, item, seq_ref, loss_ref, merged, out_grad, proj_w, proj_b, gain, shift, up_w, up_b, down_w, down_b, *rest):
    blocks = rest[:parts]
    outs = rest[parts : 2 * parts]
    (
        block_out,
        d_after_ref,
        normed_ref,
        attended_ref,
        activ_ref,
        d_pre_ref,
        down_mine,
        down_theirs,
        branch_mine,
        branch_theirs,
        up_bias_grad,
        vector_grads,
    ) = rest[2 * parts : 2 * parts + 12]
    after, low, d_down, acc_out, acc_back, wide, groups, half = rest[2 * parts + 12 :]
    step = pl.program_id(0)
    last = pl.num_programs(0) - 1
    me = seq_ref[0]
    rows, width = after.shape
    padded = normed_ref.shape[1]
    local = width // parts
    weight = loss_ref[item]

    @pl.when(step == 0)
    def _():
        for k in range(parts):
            groups[me ^ k] = blocks[k][...]
        for group in range(parts):
            wide[:, group * local : (group + 1) * local] = groups[group]
        attended = wide[...]
        store_padded(attended_ref, attended)
        hidden = merged[...] + dot(attended, proj_w[...]) + proj_b[...].astype(F32)
        after[...] = hidden
        acc_out[...] = hidden + down_b[...].astype(F32)
        acc_back[...] = jnp.zeros_like(acc_back)
        normal, _ = normalize(hidden)
        value = (normal * gain[...].astype(F32) + shift[...].astype(F32)).astype(BF16)
        low[...] = value
        store_padded(normed_ref, value)
        grad = (out_grad[0].astype(F32) * weight).astype(BF16)
        d_down[...] = grad
        vector_grads[0:1, :] = jnp.sum(grad.astype(F32), axis=0, keepdims=True)
        write_halves(grad, half, down_mine, down_theirs, me & 1, parts)

    pre_act = dot(low[...], up_w[...]) + up_b[...].astype(F32)
    d_activ = dot_t(d_down[...], down_w[...])
    phi = 0.5 + 0.5 * lax.erf(pre_act * (0.5**0.5))
    density = jnp.exp2(pre_act * pre_act * (-0.5 * LOG2E)) * ((2.0 * math.pi) ** -0.5)
    activ = (pre_act * phi).astype(BF16)
    d_pre = (d_activ * (phi + pre_act * density)).astype(BF16)
    activ_ref[0, :rows, :] = activ
    d_pre_ref[0, 0, :rows, :] = d_pre
    if padded > rows:
        activ_ref[0, rows:, :] = jnp.zeros((padded - rows, activ.shape[1]), BF16)
        d_pre_ref[0, 0, rows:, :] = jnp.zeros((padded - rows, activ.shape[1]), BF16)
    up_bias_grad[...] = jnp.sum(d_pre.astype(F32), axis=0, keepdims=True)
    acc_out[...] += dot(activ, down_w[...])
    acc_back[...] += dot_t(d_pre, up_w[...])

    @pl.when(step == last)
    def _():
        block_out[0] = acc_out[...].astype(BF16)
        normal, inverse = normalize(after[...])
        d_hidden, gain_sum, shift_sum = norm_back(acc_back[...], normal, inverse, gain[...].astype(F32))
        d_after = out_grad[0].astype(F32) * weight + d_hidden
        d_after_ref[...] = d_after
        branch = d_after.astype(BF16)
        vector_grads[1:2, :] = gain_sum
        vector_grads[2:3, :] = shift_sum
        vector_grads[3:4, :] = jnp.sum(branch.astype(F32), axis=0, keepdims=True)
        write_halves(branch, half, branch_mine, branch_theirs, me & 1, parts)
        d_attended = dot_t(branch, proj_w[...]).astype(BF16)
        for group in range(parts):
            groups[group] = d_attended[:, group * local : (group + 1) * local]
        for k in range(parts):
            outs[k][...] = groups[me ^ k]


def tail_kernel(parts, seq_ref, merged, d_after, gain, qkv_w, skip_w, *rest):
    blocks = rest[:parts]
    token_grad, skip_grad, pack_mine, pack_theirs, merge_mine, merge_theirs, vector_grads = rest[parts : parts + 7]
    acc, low, packed, groups, half, wide_half, joined = rest[parts + 7 :]
    step = pl.program_id(0)
    me = seq_ref[0]
    rows, width = acc.shape
    local = width // parts

    @pl.when(step == 0)
    def _():
        for k in range(parts):
            groups[me ^ k] = blocks[k][...]
        for which in range(3):
            for group in range(parts):
                packed[which, :, group * local : (group + 1) * local] = groups[
                    group, :, which * local : (which + 1) * local
                ]
            joined[:, which * width : (which + 1) * width] = packed[which]
        write_halves(joined[...], wide_half, pack_mine, pack_theirs, me & 1, parts)
        acc[...] = jnp.zeros_like(acc)

    @pl.when(step < 3)
    def _():
        acc[...] += dot_t(packed[step], qkv_w[...])

    @pl.when(step == 2)
    def _():
        normal, inverse = normalize(merged[...])
        d_hidden, gain_sum, shift_sum = norm_back(acc[...], normal, inverse, gain[...].astype(F32))
        d_merged = (d_after[...] + d_hidden).astype(BF16)
        low[...] = d_merged
        vector_grads[0:1, :] = gain_sum
        vector_grads[1:2, :] = shift_sum
        vector_grads[2:3, :] = jnp.sum(d_merged.astype(F32), axis=0, keepdims=True)
        vector_grads[3:4, :] = jnp.zeros_like(gain_sum)
        write_halves(d_merged, half, merge_mine, merge_theirs, me & 1, parts)

    @pl.when(step == 3)
    def _():
        token_grad[0] = dot_t(low[...], skip_w[...]).astype(BF16)

    @pl.when(step == 4)
    def _():
        skip_grad[0] = dot_t(low[...], skip_w[...]).astype(BF16)


def xor_permute(value, axis, bit):
    count = lax.axis_size(axis)
    return lax.ppermute(value, axis, [(i, i ^ bit) for i in range(count)])


def exchange(blocks):
    return [block if k == 0 else xor_permute(block, "seq", k) for k, block in enumerate(blocks)]


def bit_of(axis, bit):
    return (lax.axis_index(axis) // bit) % 2


def parity_blocks(value, block, parity):
    count = value.shape[1] // block
    return jnp.concatenate([value[:, j * block : (j + 1) * block] for j in range(parity, count, 2)], axis=1)


def scatter_sum(left, mine, theirs):
    dp, parts = lax.axis_size("dp"), lax.axis_size("seq")
    got = xor_permute(contract_rows(left, theirs).astype(BF16), "seq", 1)
    total = (contract_rows(left, mine) + got.astype(F32)).astype(BF16)
    row_block, width = total.shape[0] // dp, total.shape[1]
    total = total.reshape(dp, row_block, width)
    bit = 1
    while bit < dp:
        pairs = total.reshape(-1, 2, row_block, width)
        place = bit_of("dp", bit)
        keep = lax.dynamic_index_in_dim(pairs, place, 1, keepdims=False)
        send = lax.dynamic_index_in_dim(pairs, 1 - place, 1, keepdims=False)
        got = xor_permute(send, "dp", bit)
        total = (keep.astype(F32) + got.astype(F32)).astype(BF16)
        bit *= 2
    total = total.reshape(row_block, width)
    block = 2 * width // parts
    bit = 2
    while bit < parts:
        even, odd = parity_blocks(total, block, 0), parity_blocks(total, block, 1)
        place = bit_of("seq", bit) == 0
        keep = jnp.where(place, even, odd)
        got = xor_permute(jnp.where(place, odd, even), "seq", bit)
        result = keep.astype(F32) + got.astype(F32)
        total = result.astype(BF16)
        bit *= 2
    return result


def sum_everywhere(value):
    for axis in ("seq", "dp"):
        bit = 1
        while bit < lax.axis_size(axis):
            value = value + xor_permute(value, axis, bit)
            bit *= 2
    return value


def body(
    tokens,
    skip_tokens,
    skip_weight,
    skip_bias,
    attn_norm_gain,
    attn_norm_bias,
    qkv_weight,
    proj_weight,
    proj_bias,
    ffn_norm_gain,
    ffn_norm_bias,
    up_weight,
    up_bias,
    down_weight,
    down_bias,
    key_mask,
    timesteps,
    out_grad,
):
    items, seg, width = tokens.shape
    parts = lax.axis_size("seq")
    heads = HEADS // parts
    size = width // HEADS
    local = width // parts
    hidden = up_weight.shape[1]
    padded = -(-seg // 8) * 8
    full = seg * parts
    me = lax.axis_index("seq").astype(jnp.int32)
    seq_index = me.reshape(1)
    row = lambda v: v.reshape(1, -1)
    phase = 0.5 * math.pi * timesteps.astype(F32) / DIFF_STEPS
    loss_weight = 0.5 + jnp.cos(phase) ** 2
    order = me ^ jnp.arange(parts, dtype=jnp.int32)
    valid = jnp.take(key_mask.reshape(items, parts, seg), order, axis=1)
    bias = jnp.where(valid.reshape(items, 1, full) > 0, 0.0, -1e30).astype(F32)

    def vmem(shape, dtype):
        return pltpu.VMEM(shape, dtype)

    def at_item(item, rows, columns):
        return pl.BlockSpec((1, rows, columns), lambda *_: (item, 0, 0))

    def front(item, prev):
        blocks = [Out((seg, 3 * local), BF16, whole((seg, 3 * local))) for _ in range(parts)]
        return call(
            functools.partial(front_kernel, parts),
            "front",
            (5,),
            [seq_index],
            [
                (tokens, at_item(item, seg, width)),
                (skip_tokens, at_item(item, seg, width)),
                (skip_weight, pl.BlockSpec((width, width), lambda c, *_: (jnp.minimum(c, 1), 0))),
                (row(skip_bias), whole((1, width))),
                (row(attn_norm_gain), whole((1, width))),
                (row(attn_norm_bias), whole((1, width))),
                (qkv_weight, pl.BlockSpec((width, width), lambda c, *_: (0, jnp.maximum(c - 2, 0)))),
            ],
            blocks
            + [
                Out((seg, width), F32, whole((seg, width))),
                Out((items, padded, width), BF16, at_item(item, padded, width), prev[0]),
                Out((items, padded, 2 * width), BF16, at_item(item, padded, 2 * width), prev[1]),
            ],
            [
                vmem((seg, width), F32),
                vmem((seg, width), BF16),
                vmem((3, seg, width), BF16),
                vmem((parts, seg, 3 * local), BF16),
            ],
            2 * seg * width * width * 5,
            10 * width * width + 16 * seg * width,
        )

    def attend(item, blocks):
        return call(
            functools.partial(attend_kernel, parts, heads),
            "attend",
            (1,),
            [],
            [(bias, pl.BlockSpec((1, 1, full), lambda *_: (item, 0, 0)))]
            + [(block, whole((seg, 3 * local))) for block in blocks],
            [Out((seg, local), BF16, whole((seg, local))) for _ in range(parts)]
            + [Out((parts, seg, 128), F32, whole((parts, seg, 128)))],
            [
                vmem((parts, heads, seg, size), BF16),
                vmem((heads, full, size), BF16),
                vmem((heads, full, size), BF16),
                vmem((parts, seg, local), BF16),
            ],
            20 * heads * full * full * size,
            8 * full * local + 512 * full,
        )

    def attend_back(item, blocks, grads, log_sum):
        return call(
            functools.partial(attend_back_kernel, parts, heads),
            "attend_back",
            (1,),
            [],
            [
                (bias, pl.BlockSpec((1, 1, full), lambda *_: (item, 0, 0))),
                (log_sum, whole((parts, seg, 128))),
            ]
            + [(block, whole((seg, 3 * local))) for block in blocks]
            + [(grad, whole((seg, local))) for grad in grads],
            [Out((seg, 3 * local), BF16, whole((seg, 3 * local))) for _ in range(parts)],
            [
                vmem((parts, heads, seg, size), BF16),
                vmem((heads, full, size), BF16),
                vmem((heads, full, size), BF16),
                vmem((parts, heads, seg, size), BF16),
                vmem((parts, seg, local), BF16),
                vmem((heads, size, full), F32),
                vmem((heads, size, full), F32),
                vmem((full, size), F32),
            ],
            50 * heads * full * full * size,
            14 * full * local + 512 * full,
        )

    chunks = 4
    chunk = hidden // chunks
    direct = (hidden // parts) % chunk == 0 and parts % 2 == 0 and chunk % 128 == 0
    if direct:
        per = hidden // parts // chunk
        pre_shape = (2, items, padded, hidden // 2)

        def pre_map(item):
            return lambda c, seq: (((c // per) % 2) ^ (seq[0] & 1), item, 0, (c // per // 2) * per + c % per)
    else:
        pre_shape = (1, items, padded, hidden)

        def pre_map(item):
            return lambda c, seq: (0, item, 0, c)

    def ffn(item, merged, blocks, prev):
        half_out = lambda p: Out((items, padded, width // 2), BF16, at_item(item, padded, width // 2), p)
        return call(
            functools.partial(ffn_kernel, parts, item),
            "ffn",
            (chunks,),
            [seq_index],
            [
                (loss_weight, scalars()),
                (merged, whole((seg, width))),
                (out_grad, at_item(item, seg, width)),
                (proj_weight, whole((width, width))),
                (row(proj_bias), whole((1, width))),
                (row(ffn_norm_gain), whole((1, width))),
                (row(ffn_norm_bias), whole((1, width))),
                (up_weight, pl.BlockSpec((width, chunk), lambda c, *_: (0, c))),
                (row(up_bias), pl.BlockSpec((1, chunk), lambda c, *_: (0, c))),
                (down_weight, pl.BlockSpec((chunk, width), lambda c, *_: (c, 0))),
                (row(down_bias), whole((1, width))),
            ]
            + [(block, whole((seg, local))) for block in blocks],
            [Out((seg, local), BF16, whole((seg, local))) for _ in range(parts)]
            + [
                Out((items, seg, width), BF16, at_item(item, seg, width), prev[0]),
                Out((seg, width), F32, whole((seg, width))),
                Out((items, padded, width), BF16, at_item(item, padded, width), prev[1]),
                Out((items, padded, width), BF16, at_item(item, padded, width), prev[2]),
                Out(
                    (items, padded, hidden),
                    BF16,
                    pl.BlockSpec((1, padded, chunk), lambda c, *_: (item, 0, c)),
                    prev[3],
                ),
                Out(pre_shape, BF16, pl.BlockSpec((1, 1, padded, chunk), pre_map(item)), prev[4]),
                half_out(prev[5]),
                half_out(prev[6]),
                half_out(prev[7]),
                half_out(prev[8]),
                Out((1, hidden), F32, pl.BlockSpec((1, chunk), lambda c, *_: (0, c))),
                Out((4, width), F32, whole((4, width))),
            ],
            [
                vmem((seg, width), F32),
                vmem((seg, width), BF16),
                vmem((seg, width), BF16),
                vmem((seg, width), F32),
                vmem((seg, width), F32),
                vmem((seg, width), BF16),
                vmem((parts, seg, local), BF16),
                vmem((2, padded, width // 2), BF16),
            ],
            2 * seg * width * (4 * hidden + 2 * width),
            4 * width * hidden + 2 * width * width + 4 * seg * hidden + 24 * seg * width,
        )

    def tail(item, merged, d_after, blocks, prev):
        return call(
            functools.partial(tail_kernel, parts),
            "tail",
            (5,),
            [seq_index],
            [
                (merged, whole((seg, width))),
                (d_after, whole((seg, width))),
                (row(attn_norm_gain), whole((1, width))),
                (qkv_weight, pl.BlockSpec((width, width), lambda c, *_: (0, jnp.minimum(c, 2)))),
                (skip_weight, pl.BlockSpec((width, width), lambda c, *_: (jnp.maximum(c - 3, 0), 0))),
            ]
            + [(block, whole((seg, 3 * local))) for block in blocks],
            [
                Out((items, seg, width), BF16, at_item(item, seg, width), prev[0]),
                Out((items, seg, width), BF16, at_item(item, seg, width), prev[1]),
                Out((items, padded, 3 * width // 2), BF16, at_item(item, padded, 3 * width // 2), prev[2]),
                Out((items, padded, 3 * width // 2), BF16, at_item(item, padded, 3 * width // 2), prev[3]),
                Out((items, padded, width // 2), BF16, at_item(item, padded, width // 2), prev[4]),
                Out((items, padded, width // 2), BF16, at_item(item, padded, width // 2), prev[5]),
                Out((4, width), F32, whole((4, width))),
            ],
            [
                vmem((seg, width), F32),
                vmem((seg, width), BF16),
                vmem((3, seg, width), BF16),
                vmem((parts, seg, 3 * local), BF16),
                vmem((2, padded, width // 2), BF16),
                vmem((2, padded, 3 * width // 2), BF16),
                vmem((seg, 3 * width), BF16),
            ],
            2 * seg * width * width * 5,
            10 * width * width + 26 * seg * width,
        )

    flat = lambda v: v.reshape(items * padded, v.shape[-1])

    kept, merged_rows = [None, None], []
    head_blocks, sent = [], []
    for item in range(items):
        *blocks, merged, normed, cat = front(item, kept)
        kept = [normed, cat]
        merged_rows.append(merged)
        head_blocks.append(exchange(blocks))
    normed_attn, both_tokens = kept

    returned, log_sums = [], []
    for item in range(items):
        *outs, log_sum = attend(item, head_blocks[item])
        log_sums.append(log_sum)
        returned.append(exchange(outs))

    kept = [None] * 9
    d_heads, d_afters, up_bias_rows, vector_rows = [], [], [], []
    for item in range(items):
        results = ffn(item, merged_rows[item], returned[item], kept)
        d_heads.append(exchange(results[:parts]))
        rest = results[parts:]
        kept = [rest[0], *rest[2:10]]
        d_afters.append(rest[1])
        up_bias_rows.append(rest[10])
        vector_rows.append(rest[11])
    block_out, normed_ffn, attended, activ, d_pre, down_mine, down_theirs, branch_mine, branch_theirs = kept
    early = jnp.concatenate([sum(vector_rows), sum(up_bias_rows).reshape(-1, width)], axis=0)
    early = sum_everywhere(early)

    if direct:
        pre_mine, pre_theirs = flat(d_pre[0]), flat(d_pre[1])
    else:
        even, odd = (parity_blocks(flat(d_pre[0]), hidden // parts, p) for p in range(2))
        pre_mine, pre_theirs = (jnp.where(me % 2 == p, even, odd) for p in range(2))
    final_down = scatter_sum(flat(activ), flat(down_mine), flat(down_theirs))
    final_up = scatter_sum(flat(normed_ffn), pre_mine, pre_theirs)
    final_proj = scatter_sum(flat(attended), flat(branch_mine), flat(branch_theirs))

    d_packed = [exchange(attend_back(i, head_blocks[i], d_heads[i], log_sums[i])) for i in range(items)]

    kept = [None] * 6
    tail_rows = []
    for item in range(items):
        *kept, vectors = tail(item, merged_rows[item], d_afters[item], d_packed[item], kept)
        tail_rows.append(vectors)
    tokens_grad, skip_grad, pack_mine, pack_theirs, merge_mine, merge_theirs = kept
    late = sum_everywhere(sum(tail_rows))
    final_qkv = scatter_sum(flat(normed_attn), flat(pack_mine), flat(pack_theirs))
    final_skip = scatter_sum(flat(both_tokens), flat(merge_mine), flat(merge_theirs))
    return (
        block_out,
        tokens_grad,
        skip_grad,
        final_skip,
        final_qkv,
        final_proj,
        final_up,
        final_down,
        late[2],
        late[0],
        late[1],
        early[3],
        early[1],
        early[2],
        early[4:].reshape(-1),
        early[0],
    )


def solution(mesh):
    rows = P("dp", "seq", None)
    in_specs = (rows, rows) + (P(),) * 13 + (P("dp", None), P("dp"), rows)
    out_specs = (rows,) * 3 + (P("dp", "seq"),) * 5 + (P(),) * 8
    return jax.shard_map(body, mesh=mesh, in_specs=in_specs, out_specs=out_specs, check_vma=False)
```

```python
import functools
import math

import jax
import jax.numpy as jnp
from jax import lax
from jax.experimental import pallas as pl
from jax.experimental.layout import Layout, with_layout_constraint
from jax.experimental.pallas import tpu as pltpu
from jax.sharding import PartitionSpec as P

HEADS = 16
DIFF_STEPS = 1000
EPS = 1e-05
F32 = jnp.float32
BF16 = jnp.bfloat16
VMEM_BYTES = 63 * 1024 * 1024
LOG2E = math.log2(math.e)


def contract_rows(left, right):
    return lax.dot_general(left, right, (((0,), (0,)), ((), ())), preferred_element_type=F32)


def dot(left, right):
    return jnp.dot(left, right, preferred_element_type=F32)


def dot_t(left, right):
    return lax.dot_general(left, right, (((1,), (1,)), ((), ())), preferred_element_type=F32)


def normalize(hidden):
    centered = hidden - jnp.mean(hidden, axis=-1, keepdims=True)
    inverse = lax.rsqrt(jnp.mean(centered * centered, axis=-1, keepdims=True) + EPS)
    return (centered * inverse, inverse)


def norm_back(d_normed, normal_rows, inverse, gain):
    d_plain = d_normed * gain
    d_hidden = inverse * (
        d_plain
        - jnp.mean(d_plain, axis=-1, keepdims=True)
        - normal_rows * jnp.mean(d_plain * normal_rows, axis=-1, keepdims=True)
    )
    gain_sum = jnp.sum(d_normed * normal_rows, axis=0, keepdims=True)
    return (d_hidden, gain_sum, jnp.sum(d_normed, axis=0, keepdims=True))


def whole(shape):
    return pl.BlockSpec(shape, lambda *_: (0,) * len(shape))


def scalars():
    return pl.BlockSpec(memory_space=pltpu.SMEM)


class Out:
    def __init__(self, shape, dtype, spec, prev=None):
        self.shape, self.dtype, self.spec, self.prev = shape, dtype, spec, prev


def call(kernel, name, grid, prefetch, inputs, outs, scratch, flops, moved, after=()):
    carried = [(k, out) for k, out in enumerate(outs) if out.prev is not None]
    first_out = len(prefetch) + len(inputs)

    def body(*refs):
        kernel(*refs[:first_out], *refs[first_out + len(carried) + len(after) :])

    return pl.pallas_call(
        body,
        name=name,
        out_shape=[jax.ShapeDtypeStruct(out.shape, out.dtype) for out in outs],
        grid_spec=pltpu.PrefetchScalarGridSpec(
            num_scalar_prefetch=len(prefetch),
            grid=grid,
            in_specs=[spec for _, spec in inputs] + [pl.BlockSpec(memory_space=pl.ANY)] * (len(carried) + len(after)),
            out_specs=[out.spec for out in outs],
            scratch_shapes=scratch,
        ),
        input_output_aliases={first_out + at: k for at, (k, _) in enumerate(carried)},
        compiler_params=pltpu.CompilerParams(vmem_limit_bytes=VMEM_BYTES),
        cost_estimate=pl.CostEstimate(flops=flops, bytes_accessed=moved, transcendentals=0),
    )(*prefetch, *[array for array, _ in inputs], *[out.prev for _, out in carried], *after)


def write_halves(value, half, mine_ref, theirs_ref, core, parts):
    rows, width = value.shape
    block = width // parts
    padded = half.shape[1]
    for parity in range(2):
        for at in range(parts // 2):
            source = (2 * at + parity) * block
            half[parity, :rows, at * block : (at + 1) * block] = value[:, source : source + block]
        if padded > rows:
            half[parity, rows:, :] = jnp.zeros((padded - rows, width // 2), BF16)
    mine_ref[0] = half[core]
    theirs_ref[0] = half[1 - core]


def store_padded(ref, value):
    rows, width = value.shape
    padded = ref.shape[1]
    ref[0, :rows, :] = value
    if padded > rows:
        ref[0, rows:, :] = jnp.zeros((padded - rows, width), BF16)


def front_kernel(parts, seq_ref, tok, skp, skip_w, skip_b, gain, shift, qkv_w, *rest):
    blocks, (merged, normed, cat), (acc, low, packed, groups) = rest[:parts], rest[parts : parts + 3], rest[parts + 3 :]
    step = pl.program_id(0)
    me = seq_ref[0]
    width = acc.shape[1]
    local = width // parts

    @pl.when(step == 0)
    def _():
        acc[...] = dot(tok[0], skip_w[...])
        rows, padded = tok.shape[1], cat.shape[1]
        cat[0, :rows, :width] = tok[0]
        cat[0, :rows, width:] = skp[0]
        if padded > rows:
            cat[0, rows:, :] = jnp.zeros((padded - rows, 2 * width), BF16)

    @pl.when(step == 1)
    def _():
        hidden = acc[...] + dot(skp[0], skip_w[...]) + skip_b[...].astype(F32)
        merged[...] = hidden
        normal, _ = normalize(hidden)
        value = (normal * gain[...].astype(F32) + shift[...].astype(F32)).astype(BF16)
        low[...] = value
        store_padded(normed, value)

    @pl.when(step >= 2)
    def _():
        packed[step - 2] = dot(low[...], qkv_w[...]).astype(BF16)

    @pl.when(step == 4)
    def _():
        for group in range(parts):
            for which in range(3):
                groups[group, :, which * local : (which + 1) * local] = packed[
                    which, :, group * local : (group + 1) * local
                ]
        for k in range(parts):
            blocks[k][...] = groups[me ^ k]


def split_heads(parts, heads, blocks, offset, target):
    seg = blocks[0].shape[0]
    size = target.shape[2]
    for k in range(parts):
        for head in range(heads):
            at = offset + head * size
            target[head, k * seg : (k + 1) * seg, :] = blocks[k][:, at : at + size]


def split_rows(parts, heads, blocks, offset, target):
    size = target.shape[3]
    for k in range(parts):
        for head in range(heads):
            at = offset + head * size
            target[k, head] = blocks[k][:, at : at + size]


def attend_kernel(parts, heads, bias, *rest):
    blocks, outs, (log_sum, queries, keys, values, result) = (
        rest[:parts],
        rest[parts : 2 * parts],
        rest[2 * parts :],
    )
    size = queries.shape[3]
    local = heads * size
    seg = queries.shape[2]
    split_rows(parts, heads, blocks, 0, queries)
    split_heads(parts, heads, blocks, local, keys)
    split_heads(parts, heads, blocks, 2 * local, values)
    scale = size ** (-0.5) * LOG2E
    lane = lax.broadcasted_iota(jnp.int32, (seg, 128), 1)

    @pl.loop(0, parts)
    def _(k):
        sums = jnp.zeros((seg, 128), F32)
        for head in range(heads):
            scores = dot_t(queries[k, head], keys[head]) * scale + bias[0]
            row_max = jnp.max(scores, axis=-1, keepdims=True)
            expo = jnp.exp2(scores - row_max)
            row_sum = jnp.sum(expo, axis=-1, keepdims=True)
            output = dot(expo.astype(BF16), values[head]) / row_sum
            result[k, :, head * size : (head + 1) * size] = output.astype(BF16)
            sums = jnp.where(lane == head, row_max + jnp.log2(row_sum), sums)
        log_sum[k] = sums

    for k in range(parts):
        outs[k][...] = result[k]


def attend_back_kernel(parts, heads, bias, log_sum, *rest):
    blocks, grads, outs = rest[:parts], rest[parts : 2 * parts], rest[2 * parts : 3 * parts]
    queries, keys, values, d_out, d_query, d_key_t, d_value_t, turned = rest[3 * parts :]
    size = queries.shape[3]
    seg = queries.shape[2]
    local = heads * size
    split_rows(parts, heads, blocks, 0, queries)
    split_heads(parts, heads, blocks, local, keys)
    split_heads(parts, heads, blocks, 2 * local, values)
    split_rows(parts, heads, grads, 0, d_out)
    plain = size ** (-0.5)
    scale = plain * LOG2E
    lane = lax.broadcasted_iota(jnp.int32, (seg, 128), 1)
    d_key_t[...] = jnp.zeros_like(d_key_t)
    d_value_t[...] = jnp.zeros_like(d_value_t)

    @pl.loop(0, parts)
    def _(k):
        sums = log_sum[k]
        for head in range(heads):
            query, grad = queries[k, head], d_out[k, head]
            log_row = jnp.sum(jnp.where(lane == head, sums, 0.0), axis=-1, keepdims=True)
            scores = dot_t(query, keys[head]) * scale + bias[0]
            probs = jnp.exp2(scores - log_row)
            d_probs = dot_t(grad, values[head])
            inner = jnp.sum(probs * d_probs, axis=-1, keepdims=True)
            d_scores = (probs * (d_probs - inner)).astype(BF16)
            d_query[k, :, head * size : (head + 1) * size] = (dot(d_scores, keys[head]) * plain).astype(BF16)
            d_key_t[head] += contract_rows(query, d_scores)
            d_value_t[head] += contract_rows(grad, probs.astype(BF16))

    for k in range(parts):
        outs[k][:, :local] = d_query[k]
    for at, source, factor in ((local, d_key_t, plain), (2 * local, d_value_t, 1.0)):
        for head in range(heads):
            turned[...] = jnp.transpose(source[head]) * factor
            for k in range(parts):
                outs[k][:, at + head * size : at + (head + 1) * size] = turned[
                    k * seg : (k + 1) * seg, :
                ].astype(BF16)


def ffn_kernel(parts, item, direct, seq_ref, loss_ref, merged, out_grad, proj_w, proj_b, gain, shift, up_w, up_b, down_w, down_b, *rest):
    blocks = rest[:parts]
    outs = rest[parts : 2 * parts]
    (
        block_out,
        d_after_ref,
        normed_ref,
        attended_ref,
        activ_ref,
        pre_mine,
        pre_theirs,
        down_mine,
        down_theirs,
        branch_mine,
        branch_theirs,
        up_bias_grad,
        vector_grads,
    ) = rest[2 * parts : 2 * parts + 13]
    after, low, d_down, acc_out, acc_back, wide, groups, half = rest[2 * parts + 13 :]
    step = pl.program_id(0)
    last = pl.num_programs(0) - 1
    me = seq_ref[0]
    rows, width = after.shape
    padded = normed_ref.shape[1]
    local = width // parts
    weight = loss_ref[item]

    @pl.when(step == 0)
    def _():
        for k in range(parts):
            groups[me ^ k] = blocks[k][...]
        for group in range(parts):
            wide[:, group * local : (group + 1) * local] = groups[group]
        attended = wide[...]
        store_padded(attended_ref, attended)
        hidden = merged[...] + dot(attended, proj_w[...]) + proj_b[...].astype(F32)
        after[...] = hidden
        acc_out[...] = hidden + down_b[...].astype(F32)
        acc_back[...] = jnp.zeros_like(acc_back)
        normal, _ = normalize(hidden)
        value = (normal * gain[...].astype(F32) + shift[...].astype(F32)).astype(BF16)
        low[...] = value
        store_padded(normed_ref, value)
        grad = (out_grad[0].astype(F32) * weight).astype(BF16)
        d_down[...] = grad
        vector_grads[0:1, :] = jnp.sum(grad.astype(F32), axis=0, keepdims=True)
        write_halves(grad, half, down_mine, down_theirs, me & 1, parts)

    pre_act = dot(low[...], up_w[...]) + up_b[...].astype(F32)
    d_activ = dot_t(d_down[...], down_w[...])
    phi = 0.5 + 0.5 * lax.erf(pre_act * (0.5**0.5))
    density = jnp.exp2(pre_act * pre_act * (-0.5 * LOG2E)) * ((2.0 * math.pi) ** -0.5)
    activ = (pre_act * phi).astype(BF16)
    d_pre = (d_activ * (phi + pre_act * density)).astype(BF16)
    store_padded(activ_ref, activ)
    if direct:

        @pl.when(step < (last + 1) // 2)
        def _():
            store_padded(pre_theirs, d_pre)

        @pl.when(step >= (last + 1) // 2)
        def _():
            store_padded(pre_mine, d_pre)
    else:
        store_padded(pre_mine, d_pre)
    up_bias_grad[...] = jnp.sum(d_pre.astype(F32), axis=0, keepdims=True)
    acc_out[...] += dot(activ, down_w[...])
    acc_back[...] += dot_t(d_pre, up_w[...])

    @pl.when(step == last)
    def _():
        block_out[0] = acc_out[...].astype(BF16)
        normal, inverse = normalize(after[...])
        d_hidden, gain_sum, shift_sum = norm_back(acc_back[...], normal, inverse, gain[...].astype(F32))
        d_after = out_grad[0].astype(F32) * weight + d_hidden
        d_after_ref[...] = d_after
        branch = d_after.astype(BF16)
        vector_grads[1:2, :] = gain_sum
        vector_grads[2:3, :] = shift_sum
        vector_grads[3:4, :] = jnp.sum(branch.astype(F32), axis=0, keepdims=True)
        write_halves(branch, half, branch_mine, branch_theirs, me & 1, parts)
        d_attended = dot_t(branch, proj_w[...]).astype(BF16)
        for group in range(parts):
            groups[group] = d_attended[:, group * local : (group + 1) * local]
        for k in range(parts):
            outs[k][...] = groups[me ^ k]


def tail_kernel(parts, seq_ref, merged, d_after, gain, qkv_w, skip_w, *rest):
    blocks = rest[:parts]
    token_grad, skip_grad, pack_mine, pack_theirs, merge_mine, merge_theirs, vector_grads = rest[parts : parts + 7]
    acc, low, packed, groups, half, wide_half, joined = rest[parts + 7 :]
    step = pl.program_id(0)
    me = seq_ref[0]
    rows, width = acc.shape
    local = width // parts

    @pl.when(step == 0)
    def _():
        for k in range(parts):
            groups[me ^ k] = blocks[k][...]
        for which in range(3):
            for group in range(parts):
                packed[which, :, group * local : (group + 1) * local] = groups[
                    group, :, which * local : (which + 1) * local
                ]
            joined[:, which * width : (which + 1) * width] = packed[which]
        write_halves(joined[...], wide_half, pack_mine, pack_theirs, me & 1, parts)
        acc[...] = jnp.zeros_like(acc)

    @pl.when(step < 3)
    def _():
        acc[...] += dot_t(packed[step], qkv_w[...])

    @pl.when(step == 2)
    def _():
        normal, inverse = normalize(merged[...])
        d_hidden, gain_sum, shift_sum = norm_back(acc[...], normal, inverse, gain[...].astype(F32))
        d_merged = (d_after[...] + d_hidden).astype(BF16)
        low[...] = d_merged
        vector_grads[0:1, :] = gain_sum
        vector_grads[1:2, :] = shift_sum
        vector_grads[2:3, :] = jnp.sum(d_merged.astype(F32), axis=0, keepdims=True)
        vector_grads[3:4, :] = jnp.zeros_like(gain_sum)
        write_halves(d_merged, half, merge_mine, merge_theirs, me & 1, parts)

    @pl.when(step == 3)
    def _():
        token_grad[0] = dot_t(low[...], skip_w[...]).astype(BF16)

    @pl.when(step == 4)
    def _():
        skip_grad[0] = dot_t(low[...], skip_w[...]).astype(BF16)


def xor_permute(value, axis, bit):
    count = lax.axis_size(axis)
    return lax.ppermute(value, axis, [(i, i ^ bit) for i in range(count)])


def exchange(blocks):
    return [block if k == 0 else xor_permute(block, "seq", k) for k, block in enumerate(blocks)]


def bit_of(axis, bit):
    index = lax.axis_index(axis).astype(jnp.uint32)
    return (index >> (bit.bit_length() - 1)) & jnp.uint32(1)


def parity_blocks(value, block, parity):
    count = value.shape[1] // block
    return jnp.concatenate([value[:, j * block : (j + 1) * block] for j in range(parity, count, 2)], axis=1)


def row_major(value):
    return with_layout_constraint(value, Layout(tuple(range(value.ndim))))


class ScatterSum:
    def __init__(self, left, mine, theirs, first):
        dp = lax.axis_size("dp")
        self.row_block, self.width = left.shape[1] // dp, mine.shape[1]
        shape = (dp, self.row_block, self.width)
        got = row_major(xor_permute(row_major(contract_rows(left, theirs).astype(BF16)).reshape(shape), "seq", 1))
        got = lax.optimization_barrier(got).reshape(left.shape[1], self.width)
        total = row_major((contract_rows(left, mine) + got.astype(F32)).astype(BF16)).reshape(shape)
        self.rest = [1 << k for k in range(dp.bit_length() - 1)]
        self.order = sorted(self.rest, key=lambda bit: (bit != first, bit))
        self.split(total)

    def split(self, total):
        bit = self.order.pop(0)
        at = self.rest.index(bit)
        self.rest.remove(bit)
        pairs = total.reshape(-1, 2, self.row_block << at, self.width)
        place = bit_of("dp", bit)
        self.keep = lax.dynamic_index_in_dim(pairs, place, 1, keepdims=False)
        self.send = lax.dynamic_index_in_dim(pairs, 1 - place, 1, keepdims=False)
        self.got = xor_permute(self.send, "dp", bit)

    def advance(self):
        self.split((self.keep.astype(F32) + self.got.astype(F32)).astype(BF16))
        return self.send

    def finish(self):
        parts = lax.axis_size("seq")
        while self.order:
            self.advance()
        result = (self.keep.astype(F32) + self.got.astype(F32)).reshape(self.row_block, self.width)
        block = 2 * self.width // parts
        bit = 2
        while bit < parts:
            total = result.astype(BF16)
            even, odd = parity_blocks(total, block, 0), parity_blocks(total, block, 1)
            place = bit_of("seq", bit) == 0
            keep = jnp.where(place, even, odd)
            got = xor_permute(jnp.where(place, odd, even), "seq", bit)
            result = keep.astype(F32) + got.astype(F32)
            bit *= 2
        return result


def sum_everywhere(value):
    for axis in ("seq", "dp"):
        bit = 1
        while bit < lax.axis_size(axis):
            value = value + xor_permute(value, axis, bit)
            bit *= 2
    return value


def body(
    tokens,
    skip_tokens,
    skip_weight,
    skip_bias,
    attn_norm_gain,
    attn_norm_bias,
    qkv_weight,
    proj_weight,
    proj_bias,
    ffn_norm_gain,
    ffn_norm_bias,
    up_weight,
    up_bias,
    down_weight,
    down_bias,
    key_mask,
    timesteps,
    out_grad,
):
    items, seg, width = tokens.shape
    parts = lax.axis_size("seq")
    heads = HEADS // parts
    size = width // HEADS
    local = width // parts
    hidden = up_weight.shape[1]
    padded = -(-seg // 8) * 8
    full = seg * parts
    me = lax.axis_index("seq").astype(jnp.int32)
    seq_index = me.reshape(1)
    row = lambda v: v.reshape(1, -1)
    phase = 0.5 * math.pi * timesteps.astype(F32) / DIFF_STEPS
    loss_weight = 0.5 + jnp.cos(phase) ** 2
    order = me ^ jnp.arange(parts, dtype=jnp.int32)
    valid = jnp.take(key_mask.reshape(items, parts, seg), order, axis=1)
    bias = jnp.where(valid.reshape(items, 1, full) > 0, 0.0, -1e30).astype(F32)

    def vmem(shape, dtype):
        return pltpu.VMEM(shape, dtype)

    def at_item(item, rows, columns):
        return pl.BlockSpec((1, rows, columns), lambda *_: (item, 0, 0))

    def front(item, prev):
        blocks = [Out((seg, 3 * local), BF16, whole((seg, 3 * local))) for _ in range(parts)]
        return call(
            functools.partial(front_kernel, parts),
            "front",
            (5,),
            [seq_index],
            [
                (tokens, at_item(item, seg, width)),
                (skip_tokens, at_item(item, seg, width)),
                (skip_weight, pl.BlockSpec((width, width), lambda c, *_: (jnp.minimum(c, 1), 0))),
                (row(skip_bias), whole((1, width))),
                (row(attn_norm_gain), whole((1, width))),
                (row(attn_norm_bias), whole((1, width))),
                (qkv_weight, pl.BlockSpec((width, width), lambda c, *_: (0, jnp.maximum(c - 2, 0)))),
            ],
            blocks
            + [
                Out((seg, width), F32, whole((seg, width))),
                Out((items, padded, width), BF16, at_item(item, padded, width), prev[0]),
                Out((items, padded, 2 * width), BF16, at_item(item, padded, 2 * width), prev[1]),
            ],
            [
                vmem((seg, width), F32),
                vmem((seg, width), BF16),
                vmem((3, seg, width), BF16),
                vmem((parts, seg, 3 * local), BF16),
            ],
            2 * seg * width * width * 5,
            10 * width * width + 16 * seg * width,
        )

    def attend(item, blocks):
        return call(
            functools.partial(attend_kernel, parts, heads),
            "attend",
            (1,),
            [],
            [(bias, pl.BlockSpec((1, 1, full), lambda *_: (item, 0, 0)))]
            + [(block, whole((seg, 3 * local))) for block in blocks],
            [Out((seg, local), BF16, whole((seg, local))) for _ in range(parts)]
            + [Out((parts, seg, 128), F32, whole((parts, seg, 128)))],
            [
                vmem((parts, heads, seg, size), BF16),
                vmem((heads, full, size), BF16),
                vmem((heads, full, size), BF16),
                vmem((parts, seg, local), BF16),
            ],
            20 * heads * full * full * size,
            8 * full * local + 512 * full,
        )

    def attend_back(item, blocks, grads, log_sum, after):
        return call(
            functools.partial(attend_back_kernel, parts, heads),
            "attend_back",
            (1,),
            [],
            [
                (bias, pl.BlockSpec((1, 1, full), lambda *_: (item, 0, 0))),
                (log_sum, whole((parts, seg, 128))),
            ]
            + [(block, whole((seg, 3 * local))) for block in blocks]
            + [(grad, whole((seg, local))) for grad in grads],
            [Out((seg, 3 * local), BF16, whole((seg, 3 * local))) for _ in range(parts)],
            [
                vmem((parts, heads, seg, size), BF16),
                vmem((heads, full, size), BF16),
                vmem((heads, full, size), BF16),
                vmem((parts, heads, seg, size), BF16),
                vmem((parts, seg, local), BF16),
                vmem((heads, size, full), F32),
                vmem((heads, size, full), F32),
                vmem((full, size), F32),
            ],
            50 * heads * full * full * size,
            14 * full * local + 512 * full,
            after,
        )

    chunks = 4
    chunk = hidden // chunks
    direct = parts == chunks and chunk % 128 == 0
    half_steps = chunks // 2

    def chunk_of(c, seq):
        if not direct:
            return c
        core = seq[0] & 1
        return jnp.where(c < half_steps, 2 * c + 1 - core, 2 * (c - half_steps) + core)

    def pre_spec(item, mine):
        if not direct:
            return pl.BlockSpec((1, padded, chunk), lambda c, *_: (item, 0, c if mine else 0))
        if mine:
            return pl.BlockSpec((1, padded, chunk), lambda c, *_: (item, 0, jnp.maximum(c - half_steps, 0)))
        return pl.BlockSpec((1, padded, chunk), lambda c, *_: (item, 0, jnp.minimum(c, half_steps - 1)))

    pre_mine_shape = (items, padded, hidden // 2 if direct else hidden)
    pre_theirs_shape = (items, padded, hidden // 2 if direct else chunk)

    def ffn(item, merged, blocks, prev):
        half_out = lambda p: Out((items, padded, width // 2), BF16, at_item(item, padded, width // 2), p)
        return call(
            functools.partial(ffn_kernel, parts, item, direct),
            "ffn",
            (chunks,),
            [seq_index],
            [
                (loss_weight, scalars()),
                (merged, whole((seg, width))),
                (out_grad, at_item(item, seg, width)),
                (proj_weight, whole((width, width))),
                (row(proj_bias), whole((1, width))),
                (row(ffn_norm_gain), whole((1, width))),
                (row(ffn_norm_bias), whole((1, width))),
                (up_weight, pl.BlockSpec((width, chunk), lambda c, seq: (0, chunk_of(c, seq)))),
                (row(up_bias), pl.BlockSpec((1, chunk), lambda c, seq: (0, chunk_of(c, seq)))),
                (down_weight, pl.BlockSpec((chunk, width), lambda c, seq: (chunk_of(c, seq), 0))),
                (row(down_bias), whole((1, width))),
            ]
            + [(block, whole((seg, local))) for block in blocks],
            [Out((seg, local), BF16, whole((seg, local))) for _ in range(parts)]
            + [
                Out((items, seg, width), BF16, at_item(item, seg, width), prev[0]),
                Out((seg, width), F32, whole((seg, width))),
                Out((items, padded, width), BF16, at_item(item, padded, width), prev[1]),
                Out((items, padded, width), BF16, at_item(item, padded, width), prev[2]),
                Out(
                    (items, padded, hidden),
                    BF16,
                    pl.BlockSpec((1, padded, chunk), lambda c, seq: (item, 0, chunk_of(c, seq))),
                    prev[3],
                ),
                Out(pre_mine_shape, BF16, pre_spec(item, True), prev[4]),
                Out(pre_theirs_shape, BF16, pre_spec(item, False), prev[5]),
                half_out(prev[6]),
                half_out(prev[7]),
                half_out(prev[8]),
                half_out(prev[9]),
                Out((1, hidden), F32, pl.BlockSpec((1, chunk), lambda c, seq: (0, chunk_of(c, seq)))),
                Out((4, width), F32, whole((4, width))),
            ],
            [
                vmem((seg, width), F32),
                vmem((seg, width), BF16),
                vmem((seg, width), BF16),
                vmem((seg, width), F32),
                vmem((seg, width), F32),
                vmem((seg, width), BF16),
                vmem((parts, seg, local), BF16),
                vmem((2, padded, width // 2), BF16),
            ],
            2 * seg * width * (4 * hidden + 2 * width),
            4 * width * hidden + 2 * width * width + 4 * seg * hidden + 24 * seg * width,
        )

    def tail(item, merged, d_after, blocks, prev, after):
        return call(
            functools.partial(tail_kernel, parts),
            "tail",
            (5,),
            [seq_index],
            [
                (merged, whole((seg, width))),
                (d_after, whole((seg, width))),
                (row(attn_norm_gain), whole((1, width))),
                (qkv_weight, pl.BlockSpec((width, width), lambda c, *_: (0, jnp.minimum(c, 2)))),
                (skip_weight, pl.BlockSpec((width, width), lambda c, *_: (jnp.maximum(c - 3, 0), 0))),
            ]
            + [(block, whole((seg, 3 * local))) for block in blocks],
            [
                Out((items, seg, width), BF16, at_item(item, seg, width), prev[0]),
                Out((items, seg, width), BF16, at_item(item, seg, width), prev[1]),
                Out((items, padded, 3 * width // 2), BF16, at_item(item, padded, 3 * width // 2), prev[2]),
                Out((items, padded, 3 * width // 2), BF16, at_item(item, padded, 3 * width // 2), prev[3]),
                Out((items, padded, width // 2), BF16, at_item(item, padded, width // 2), prev[4]),
                Out((items, padded, width // 2), BF16, at_item(item, padded, width // 2), prev[5]),
                Out((4, width), F32, whole((4, width))),
            ],
            [
                vmem((seg, width), F32),
                vmem((seg, width), BF16),
                vmem((3, seg, width), BF16),
                vmem((parts, seg, 3 * local), BF16),
                vmem((2, padded, width // 2), BF16),
                vmem((2, padded, 3 * width // 2), BF16),
                vmem((seg, 3 * width), BF16),
            ],
            2 * seg * width * width * 5,
            10 * width * width + 26 * seg * width,
            after,
        )

    flat = lambda v: v.reshape(items * padded, v.shape[-1])

    kept, merged_rows = [None, None], []
    head_blocks, sent = [], []
    for item in range(items):
        *blocks, merged, normed, cat = front(item, kept)
        kept = [normed, cat]
        merged_rows.append(merged)
        head_blocks.append(exchange(blocks))
    normed_attn, both_tokens = kept

    returned, log_sums = [], []
    for item in range(items):
        *outs, log_sum = attend(item, head_blocks[item])
        log_sums.append(log_sum)
        returned.append(exchange(outs))

    kept = [None] * 10
    d_heads, d_afters, up_bias_rows, vector_rows = [], [], [], []
    for item in range(items):
        results = ffn(item, merged_rows[item], returned[item], kept)
        d_heads.append(exchange(results[:parts]))
        rest = results[parts:]
        kept = [rest[0], *rest[2:11]]
        d_afters.append(rest[1])
        up_bias_rows.append(rest[11])
        vector_rows.append(rest[12])
    block_out, normed_ffn, attended, activ, pre_mine, pre_theirs, down_mine, down_theirs, branch_mine, branch_theirs = kept
    if direct:
        pre_mine, pre_theirs = flat(pre_mine), flat(pre_theirs)
    else:
        even, odd = (parity_blocks(flat(pre_mine), hidden // parts, p) for p in range(2))
        pre_mine, pre_theirs = (jnp.where(me % 2 == p, even, odd) for p in range(2))
    down = ScatterSum(flat(activ), flat(down_mine), flat(down_theirs), 1)
    up = ScatterSum(flat(normed_ffn), pre_mine, pre_theirs, 2)
    proj = ScatterSum(flat(attended), flat(branch_mine), flat(branch_theirs), 1)

    d_packed = []
    for item in range(items):
        after = []
        if item == 0:
            after = [down.send, up.send, proj.send]
        if item == items - 1:
            after = [down.advance(), up.advance()]
        d_packed.append(
            exchange(attend_back(item, head_blocks[item], d_heads[item], log_sums[item], after))
        )

    kept = [None] * 6
    tail_rows = []
    for item in range(items):
        after = [down.advance(), up.advance(), proj.advance()] if item == 1 else []
        *kept, vectors = tail(item, merged_rows[item], d_afters[item], d_packed[item], kept, after)
        tail_rows.append(vectors)
    tokens_grad, skip_grad, pack_mine, pack_theirs, merge_mine, merge_theirs = kept
    vectors = sum_everywhere(
        jnp.concatenate([sum(tail_rows), sum(vector_rows), sum(up_bias_rows).reshape(-1, width)], axis=0)
    )
    late, early = vectors[:4], vectors[4:]
    qkv = ScatterSum(flat(normed_attn), flat(pack_mine), flat(pack_theirs), 1)
    skip = ScatterSum(flat(both_tokens), flat(merge_mine), flat(merge_theirs), 2)
    final_down, final_up, final_proj = down.finish(), up.finish(), proj.finish()
    final_qkv, final_skip = qkv.finish(), skip.finish()
    return (
        block_out,
        tokens_grad,
        skip_grad,
        final_skip,
        final_qkv,
        final_proj,
        final_up,
        final_down,
        late[2],
        late[0],
        late[1],
        early[3],
        early[1],
        early[2],
        early[4:].reshape(-1),
        early[0],
    )


def solution(mesh):
    rows = P("dp", "seq", None)
    in_specs = (rows, rows) + (P(),) * 13 + (P("dp", None), P("dp"), rows)
    out_specs = (rows,) * 3 + (P("dp", "seq"),) * 5 + (P(),) * 8
    return jax.shard_map(body, mesh=mesh, in_specs=in_specs, out_specs=out_specs, check_vma=False)
```

```python
import functools
import math

import jax
import jax.numpy as jnp
from jax import lax
from jax.experimental import pallas as pl
from jax.experimental.layout import Layout, with_layout_constraint
from jax.experimental.pallas import tpu as pltpu
from jax.sharding import PartitionSpec as P

HEADS = 16
DIFF_STEPS = 1000
EPS = 1e-05
F32 = jnp.float32
BF16 = jnp.bfloat16
VMEM_BYTES = 63 * 1024 * 1024
LOG2E = math.log2(math.e)


def contract_rows(left, right):
    return lax.dot_general(left, right, (((0,), (0,)), ((), ())), preferred_element_type=F32)


def dot(left, right):
    return jnp.dot(left, right, preferred_element_type=F32)


def dot_t(left, right):
    return lax.dot_general(left, right, (((1,), (1,)), ((), ())), preferred_element_type=F32)


def normalize(hidden):
    centered = hidden - jnp.mean(hidden, axis=-1, keepdims=True)
    inverse = lax.rsqrt(jnp.mean(centered * centered, axis=-1, keepdims=True) + EPS)
    return (centered * inverse, inverse)


def norm_back(d_normed, normal_rows, inverse, gain):
    d_plain = d_normed * gain
    d_hidden = inverse * (
        d_plain
        - jnp.mean(d_plain, axis=-1, keepdims=True)
        - normal_rows * jnp.mean(d_plain * normal_rows, axis=-1, keepdims=True)
    )
    gain_sum = jnp.sum(d_normed * normal_rows, axis=0, keepdims=True)
    return (d_hidden, gain_sum, jnp.sum(d_normed, axis=0, keepdims=True))


def whole(shape):
    return pl.BlockSpec(shape, lambda *_: (0,) * len(shape))


def scalars():
    return pl.BlockSpec(memory_space=pltpu.SMEM)


class Out:
    def __init__(self, shape, dtype, spec, prev=None):
        self.shape, self.dtype, self.spec, self.prev = shape, dtype, spec, prev


def call(kernel, name, grid, prefetch, inputs, outs, scratch, flops, moved, after=()):
    carried = [(k, out) for k, out in enumerate(outs) if out.prev is not None]
    first_out = len(prefetch) + len(inputs)

    def body(*refs):
        kernel(*refs[:first_out], *refs[first_out + len(carried) + len(after) :])

    return pl.pallas_call(
        body,
        name=name,
        out_shape=[jax.ShapeDtypeStruct(out.shape, out.dtype) for out in outs],
        grid_spec=pltpu.PrefetchScalarGridSpec(
            num_scalar_prefetch=len(prefetch),
            grid=grid,
            in_specs=[spec for _, spec in inputs] + [pl.BlockSpec(memory_space=pl.ANY)] * (len(carried) + len(after)),
            out_specs=[out.spec for out in outs],
            scratch_shapes=scratch,
        ),
        input_output_aliases={first_out + at: k for at, (k, _) in enumerate(carried)},
        compiler_params=pltpu.CompilerParams(vmem_limit_bytes=VMEM_BYTES),
        cost_estimate=pl.CostEstimate(flops=flops, bytes_accessed=moved, transcendentals=0),
    )(*prefetch, *[array for array, _ in inputs], *[out.prev for _, out in carried], *after)


def write_halves(value, half, mine_ref, theirs_ref, core, parts):
    rows, width = value.shape
    block = width // parts
    padded = half.shape[1]
    for parity in range(2):
        for at in range(parts // 2):
            source = (2 * at + parity) * block
            half[parity, :rows, at * block : (at + 1) * block] = value[:, source : source + block]
        if padded > rows:
            half[parity, rows:, :] = jnp.zeros((padded - rows, width // 2), BF16)
    mine_ref[0] = half[core]
    theirs_ref[0] = half[1 - core]


def store_padded(ref, value):
    rows, width = value.shape
    padded = ref.shape[1]
    ref[0, :rows, :] = value
    if padded > rows:
        ref[0, rows:, :] = jnp.zeros((padded - rows, width), BF16)


def front_kernel(parts, seq_ref, tok, skp, skip_w, skip_b, gain, shift, qkv_w, *rest):
    blocks, (merged, normed, cat), (acc, low, packed, groups) = rest[:parts], rest[parts : parts + 3], rest[parts + 3 :]
    step = pl.program_id(0)
    me = seq_ref[0]
    width = acc.shape[1]
    local = width // parts

    @pl.when(step == 0)
    def _():
        acc[...] = dot(tok[0], skip_w[...])
        rows, padded = tok.shape[1], cat.shape[1]
        cat[0, :rows, :width] = tok[0]
        cat[0, :rows, width:] = skp[0]
        if padded > rows:
            cat[0, rows:, :] = jnp.zeros((padded - rows, 2 * width), BF16)

    @pl.when(step == 1)
    def _():
        hidden = acc[...] + dot(skp[0], skip_w[...]) + skip_b[...].astype(F32)
        merged[...] = hidden
        normal, _ = normalize(hidden)
        value = (normal * gain[...].astype(F32) + shift[...].astype(F32)).astype(BF16)
        low[...] = value
        store_padded(normed, value)

    @pl.when(step >= 2)
    def _():
        packed[step - 2] = dot(low[...], qkv_w[...]).astype(BF16)

    @pl.when(step == 4)
    def _():
        for group in range(parts):
            for which in range(3):
                groups[group, :, which * local : (which + 1) * local] = packed[
                    which, :, group * local : (group + 1) * local
                ]
        for k in range(parts):
            blocks[k][...] = groups[me ^ k]


def split_heads(parts, heads, blocks, offset, target):
    seg = blocks[0].shape[0]
    size = target.shape[2]
    for k in range(parts):
        for head in range(heads):
            at = offset + head * size
            target[head, k * seg : (k + 1) * seg, :] = blocks[k][:, at : at + size]


def split_rows(parts, heads, blocks, offset, target):
    size = target.shape[3]
    for k in range(parts):
        for head in range(heads):
            at = offset + head * size
            target[k, head] = blocks[k][:, at : at + size]


def attend_kernel(parts, heads, bias, *rest):
    blocks, outs, (log_sum, queries, keys, values, result) = (
        rest[:parts],
        rest[parts : 2 * parts],
        rest[2 * parts :],
    )
    size = queries.shape[3]
    local = heads * size
    seg = queries.shape[2]
    split_rows(parts, heads, blocks, 0, queries)
    split_heads(parts, heads, blocks, local, keys)
    split_heads(parts, heads, blocks, 2 * local, values)
    scale = size ** (-0.5) * LOG2E
    lane = lax.broadcasted_iota(jnp.int32, (seg, 128), 1)

    @pl.loop(0, parts)
    def _(k):
        sums = jnp.zeros((seg, 128), F32)
        for head in range(heads):
            scores = dot_t(queries[k, head], keys[head]) * scale + bias[0]
            row_max = jnp.max(scores, axis=-1, keepdims=True)
            expo = jnp.exp2(scores - row_max)
            row_sum = jnp.sum(expo, axis=-1, keepdims=True)
            output = dot(expo.astype(BF16), values[head]) / row_sum
            result[k, :, head * size : (head + 1) * size] = output.astype(BF16)
            sums = jnp.where(lane == head, row_max + jnp.log2(row_sum), sums)
        log_sum[k] = sums

    for k in range(parts):
        outs[k][...] = result[k]


def attend_back_kernel(parts, heads, bias, log_sum, *rest):
    blocks, grads, outs = rest[:parts], rest[parts : 2 * parts], rest[2 * parts : 3 * parts]
    queries, keys, values, d_out, d_query, d_key_t, d_value_t, turned = rest[3 * parts :]
    size = queries.shape[3]
    seg = queries.shape[2]
    local = heads * size
    split_rows(parts, heads, blocks, 0, queries)
    split_heads(parts, heads, blocks, local, keys)
    split_heads(parts, heads, blocks, 2 * local, values)
    split_rows(parts, heads, grads, 0, d_out)
    plain = size ** (-0.5)
    scale = plain * LOG2E
    lane = lax.broadcasted_iota(jnp.int32, (seg, 128), 1)
    d_key_t[...] = jnp.zeros_like(d_key_t)
    d_value_t[...] = jnp.zeros_like(d_value_t)

    @pl.loop(0, parts)
    def _(k):
        sums = log_sum[k]
        for head in range(heads):
            query, grad = queries[k, head], d_out[k, head]
            log_row = jnp.sum(jnp.where(lane == head, sums, 0.0), axis=-1, keepdims=True)
            scores = dot_t(query, keys[head]) * scale + bias[0]
            probs = jnp.exp2(scores - log_row)
            d_probs = dot_t(grad, values[head])
            inner = jnp.sum(probs * d_probs, axis=-1, keepdims=True)
            d_scores = (probs * (d_probs - inner)).astype(BF16)
            d_query[k, :, head * size : (head + 1) * size] = (dot(d_scores, keys[head]) * plain).astype(BF16)
            d_key_t[head] += contract_rows(query, d_scores)
            d_value_t[head] += contract_rows(grad, probs.astype(BF16))

    for k in range(parts):
        outs[k][:, :local] = d_query[k]
    for at, source, factor in ((local, d_key_t, plain), (2 * local, d_value_t, 1.0)):
        for head in range(heads):
            turned[...] = jnp.transpose(source[head]) * factor
            for k in range(parts):
                outs[k][:, at + head * size : at + (head + 1) * size] = turned[
                    k * seg : (k + 1) * seg, :
                ].astype(BF16)


def ffn_kernel(parts, item, direct, seq_ref, loss_ref, merged, out_grad, proj_w, proj_b, gain, shift, up_w, up_b, down_w, down_b, *rest):
    blocks = rest[:parts]
    outs = rest[parts : 2 * parts]
    (
        block_out,
        d_after_ref,
        normed_ref,
        attended_ref,
        activ_ref,
        pre_mine,
        pre_theirs,
        down_mine,
        down_theirs,
        branch_mine,
        branch_theirs,
        up_bias_grad,
        vector_grads,
    ) = rest[2 * parts : 2 * parts + 13]
    after, low, d_down, acc_out, acc_back, wide, groups, half = rest[2 * parts + 13 :]
    step = pl.program_id(0)
    last = pl.num_programs(0) - 1
    me = seq_ref[0]
    rows, width = after.shape
    padded = normed_ref.shape[1]
    local = width // parts
    weight = loss_ref[item]

    @pl.when(step == 0)
    def _():
        for k in range(parts):
            groups[me ^ k] = blocks[k][...]
        for group in range(parts):
            wide[:, group * local : (group + 1) * local] = groups[group]
        attended = wide[...]
        store_padded(attended_ref, attended)
        hidden = merged[...] + dot(attended, proj_w[...]) + proj_b[...].astype(F32)
        after[...] = hidden
        acc_out[...] = hidden + down_b[...].astype(F32)
        acc_back[...] = jnp.zeros_like(acc_back)
        normal, _ = normalize(hidden)
        value = (normal * gain[...].astype(F32) + shift[...].astype(F32)).astype(BF16)
        low[...] = value
        store_padded(normed_ref, value)
        grad = (out_grad[0].astype(F32) * weight).astype(BF16)
        d_down[...] = grad
        vector_grads[0:1, :] = jnp.sum(grad.astype(F32), axis=0, keepdims=True)
        write_halves(grad, half, down_mine, down_theirs, me & 1, parts)

    pre_act = dot(low[...], up_w[...]) + up_b[...].astype(F32)
    d_activ = dot_t(d_down[...], down_w[...])
    phi = 0.5 + 0.5 * lax.erf(pre_act * (0.5**0.5))
    density = jnp.exp2(pre_act * pre_act * (-0.5 * LOG2E)) * ((2.0 * math.pi) ** -0.5)
    activ = (pre_act * phi).astype(BF16)
    d_pre = (d_activ * (phi + pre_act * density)).astype(BF16)
    store_padded(activ_ref, activ)
    if direct:

        @pl.when(step < (last + 1) // 2)
        def _():
            store_padded(pre_theirs, d_pre)

        @pl.when(step >= (last + 1) // 2)
        def _():
            store_padded(pre_mine, d_pre)
    else:
        store_padded(pre_mine, d_pre)
    up_bias_grad[...] = jnp.sum(d_pre.astype(F32), axis=0, keepdims=True)
    acc_out[...] += dot(activ, down_w[...])
    acc_back[...] += dot_t(d_pre, up_w[...])

    @pl.when(step == last)
    def _():
        block_out[0] = acc_out[...].astype(BF16)
        normal, inverse = normalize(after[...])
        d_hidden, gain_sum, shift_sum = norm_back(acc_back[...], normal, inverse, gain[...].astype(F32))
        d_after = out_grad[0].astype(F32) * weight + d_hidden
        d_after_ref[...] = d_after
        branch = d_after.astype(BF16)
        vector_grads[1:2, :] = gain_sum
        vector_grads[2:3, :] = shift_sum
        vector_grads[3:4, :] = jnp.sum(branch.astype(F32), axis=0, keepdims=True)
        write_halves(branch, half, branch_mine, branch_theirs, me & 1, parts)
        d_attended = dot_t(branch, proj_w[...]).astype(BF16)
        for group in range(parts):
            groups[group] = d_attended[:, group * local : (group + 1) * local]
        for k in range(parts):
            outs[k][...] = groups[me ^ k]


def tail_kernel(parts, seq_ref, merged, d_after, gain, qkv_w, *rest):
    blocks = rest[:parts]
    d_merged_ref, pack_mine, pack_theirs, merge_mine, merge_theirs, vector_grads = rest[parts : parts + 6]
    acc, packed, groups, half, wide_half, joined = rest[parts + 6 :]
    step = pl.program_id(0)
    me = seq_ref[0]
    rows, width = acc.shape
    local = width // parts

    @pl.when(step == 0)
    def _():
        for k in range(parts):
            groups[me ^ k] = blocks[k][...]
        for which in range(3):
            for group in range(parts):
                packed[which, :, group * local : (group + 1) * local] = groups[
                    group, :, which * local : (which + 1) * local
                ]
            joined[:, which * width : (which + 1) * width] = packed[which]
        write_halves(joined[...], wide_half, pack_mine, pack_theirs, me & 1, parts)
        acc[...] = jnp.zeros_like(acc)

    acc[...] += dot_t(packed[step], qkv_w[...])

    @pl.when(step == 2)
    def _():
        normal, inverse = normalize(merged[...])
        d_hidden, gain_sum, shift_sum = norm_back(acc[...], normal, inverse, gain[...].astype(F32))
        d_merged = (d_after[...] + d_hidden).astype(BF16)
        d_merged_ref[0] = d_merged
        vector_grads[0:1, :] = gain_sum
        vector_grads[1:2, :] = shift_sum
        vector_grads[2:3, :] = jnp.sum(d_merged.astype(F32), axis=0, keepdims=True)
        vector_grads[3:4, :] = jnp.zeros_like(gain_sum)
        write_halves(d_merged, half, merge_mine, merge_theirs, me & 1, parts)


def input_grads_kernel(d_merged, skip_w, token_grad, skip_grad):
    value = dot_t(d_merged[0], skip_w[...]).astype(BF16)

    @pl.when(pl.program_id(0) == 0)
    def _():
        token_grad[0] = value

    @pl.when(pl.program_id(0) == 1)
    def _():
        skip_grad[0] = value


def xor_permute(value, axis, bit):
    count = lax.axis_size(axis)
    return lax.ppermute(value, axis, [(i, i ^ bit) for i in range(count)])


def exchange(blocks):
    return [block if k == 0 else xor_permute(block, "seq", k) for k, block in enumerate(blocks)]


def bit_of(axis, bit):
    index = lax.axis_index(axis).astype(jnp.uint32)
    return (index >> (bit.bit_length() - 1)) & jnp.uint32(1)


def parity_blocks(value, block, parity):
    count = value.shape[-1] // block
    return jnp.concatenate([value[..., j * block : (j + 1) * block] for j in range(parity, count, 2)], axis=-1)


def row_major(value):
    return with_layout_constraint(value, Layout(tuple(range(value.ndim))))


def tie(value, *others):
    return lax.optimization_barrier((value, *others))[0]


def axis_bits(axis, lowest=1):
    return [(axis, 1 << k) for k in range(lax.axis_size(axis).bit_length() - 1) if 1 << k >= lowest]


class Flow:
    def __init__(self, total, order):
        self.blocks = [bit for _, bit in axis_bits("dp")]
        everything = axis_bits("dp") + axis_bits("seq", 2)
        self.order = [step for step in order if step in everything]
        self.order += [step for step in everything if step not in self.order]
        self.split(total)

    def split(self, total):
        axis, bit = self.order.pop(0)
        place = bit_of(axis, bit)
        if axis == "dp":
            at = self.blocks.index(bit)
            self.blocks.remove(bit)
            count, rows, width = total.shape
            pairs = total.reshape(count >> (at + 1), 2, 1 << at, rows, width)
            self.keep, self.send = (
                lax.dynamic_index_in_dim(pairs, which, 1, keepdims=False).reshape(count // 2, rows, width)
                for which in (place, 1 - place)
            )
        else:
            block = 2 * self.width(total) // lax.axis_size("seq")
            even, odd = (parity_blocks(total, block, parity) for parity in range(2))
            self.keep = jnp.where(place == 0, even, odd)
            self.send = jnp.where(place == 0, odd, even)
        self.got = xor_permute(self.send, axis, bit)

    def width(self, total):
        done = len(axis_bits("seq", 2)) - 1 - sum(axis == "seq" for axis, _ in self.order)
        return total.shape[2] << done

    def advance(self, *after):
        keep = tie(self.keep, *after) if after else self.keep
        self.split((keep.astype(F32) + self.got.astype(F32)).astype(BF16))
        return self.send

    def finish(self):
        while self.order:
            self.advance()
        return (self.keep.astype(F32) + self.got.astype(F32))[0]


class ScatterSum:
    def __init__(self, left, theirs):
        self.left = left
        self.shape = (lax.axis_size("dp"), left.shape[1] // lax.axis_size("dp"), theirs.shape[1])
        self.sent = row_major(contract_rows(left, theirs).astype(BF16)).reshape(self.shape)
        self.got = xor_permute(self.sent, "seq", 1)

    def join(self, mine, *flows):
        got = lax.optimization_barrier(row_major(self.got)).reshape(self.left.shape[1], mine.shape[1])
        total = row_major((contract_rows(self.left, mine) + got.astype(F32)).astype(BF16)).reshape(self.shape)
        self.flows, start = [], 0
        for k, (share, order) in enumerate(flows):
            end = start + int(self.shape[1] * share) // 16 * 16 if k < len(flows) - 1 else self.shape[1]
            self.flows.append(Flow(total[:, start:end], order))
            start = end
        return [flow.send for flow in self.flows]

    def advance(self, *after):
        return [flow.advance(*after) for flow in self.flows]

    def finish(self):
        return jnp.concatenate([flow.finish() for flow in self.flows], axis=0)


def body(
    tokens,
    skip_tokens,
    skip_weight,
    skip_bias,
    attn_norm_gain,
    attn_norm_bias,
    qkv_weight,
    proj_weight,
    proj_bias,
    ffn_norm_gain,
    ffn_norm_bias,
    up_weight,
    up_bias,
    down_weight,
    down_bias,
    key_mask,
    timesteps,
    out_grad,
):
    items, seg, width = tokens.shape
    parts = lax.axis_size("seq")
    heads = HEADS // parts
    size = width // HEADS
    local = width // parts
    hidden = up_weight.shape[1]
    padded = -(-seg // 8) * 8
    full = seg * parts
    me = lax.axis_index("seq").astype(jnp.int32)
    seq_index = me.reshape(1)
    row = lambda v: v.reshape(1, -1)
    phase = 0.5 * math.pi * timesteps.astype(F32) / DIFF_STEPS
    loss_weight = 0.5 + jnp.cos(phase) ** 2
    order = me ^ jnp.arange(parts, dtype=jnp.int32)
    valid = jnp.take(key_mask.reshape(items, parts, seg), order, axis=1)
    bias = jnp.where(valid.reshape(items, 1, full) > 0, 0.0, -1e30).astype(F32)

    def vmem(shape, dtype):
        return pltpu.VMEM(shape, dtype)

    def at_item(item, rows, columns):
        return pl.BlockSpec((1, rows, columns), lambda *_: (item, 0, 0))

    def front(item, prev):
        blocks = [Out((seg, 3 * local), BF16, whole((seg, 3 * local))) for _ in range(parts)]
        return call(
            functools.partial(front_kernel, parts),
            "front",
            (5,),
            [seq_index],
            [
                (tokens, at_item(item, seg, width)),
                (skip_tokens, at_item(item, seg, width)),
                (skip_weight, pl.BlockSpec((width, width), lambda c, *_: (jnp.minimum(c, 1), 0))),
                (row(skip_bias), whole((1, width))),
                (row(attn_norm_gain), whole((1, width))),
                (row(attn_norm_bias), whole((1, width))),
                (qkv_weight, pl.BlockSpec((width, width), lambda c, *_: (0, jnp.maximum(c - 2, 0)))),
            ],
            blocks
            + [
                Out((seg, width), F32, whole((seg, width))),
                Out((items, padded, width), BF16, at_item(item, padded, width), prev[0]),
                Out((items, padded, 2 * width), BF16, at_item(item, padded, 2 * width), prev[1]),
            ],
            [
                vmem((seg, width), F32),
                vmem((seg, width), BF16),
                vmem((3, seg, width), BF16),
                vmem((parts, seg, 3 * local), BF16),
            ],
            2 * seg * width * width * 5,
            10 * width * width + 16 * seg * width,
        )

    def attend(item, blocks):
        return call(
            functools.partial(attend_kernel, parts, heads),
            "attend",
            (1,),
            [],
            [(bias, pl.BlockSpec((1, 1, full), lambda *_: (item, 0, 0)))]
            + [(block, whole((seg, 3 * local))) for block in blocks],
            [Out((seg, local), BF16, whole((seg, local))) for _ in range(parts)]
            + [Out((parts, seg, 128), F32, whole((parts, seg, 128)))],
            [
                vmem((parts, heads, seg, size), BF16),
                vmem((heads, full, size), BF16),
                vmem((heads, full, size), BF16),
                vmem((parts, seg, local), BF16),
            ],
            20 * heads * full * full * size,
            8 * full * local + 512 * full,
        )

    def attend_back(item, blocks, grads, log_sum, after):
        return call(
            functools.partial(attend_back_kernel, parts, heads),
            "attend_back",
            (1,),
            [],
            [
                (bias, pl.BlockSpec((1, 1, full), lambda *_: (item, 0, 0))),
                (log_sum, whole((parts, seg, 128))),
            ]
            + [(block, whole((seg, 3 * local))) for block in blocks]
            + [(grad, whole((seg, local))) for grad in grads],
            [Out((seg, 3 * local), BF16, whole((seg, 3 * local))) for _ in range(parts)],
            [
                vmem((parts, heads, seg, size), BF16),
                vmem((heads, full, size), BF16),
                vmem((heads, full, size), BF16),
                vmem((parts, heads, seg, size), BF16),
                vmem((parts, seg, local), BF16),
                vmem((heads, size, full), F32),
                vmem((heads, size, full), F32),
                vmem((full, size), F32),
            ],
            50 * heads * full * full * size,
            14 * full * local + 512 * full,
            after,
        )

    chunks = 4
    chunk = hidden // chunks
    direct = parts == chunks and chunk % 128 == 0
    half_steps = chunks // 2

    def chunk_of(c, seq):
        if not direct:
            return c
        core = seq[0] & 1
        return jnp.where(c < half_steps, 2 * c + 1 - core, 2 * (c - half_steps) + core)

    def pre_spec(item, mine):
        if not direct:
            return pl.BlockSpec((1, padded, chunk), lambda c, *_: (item, 0, c if mine else 0))
        if mine:
            return pl.BlockSpec((1, padded, chunk), lambda c, *_: (item, 0, jnp.maximum(c - half_steps, 0)))
        return pl.BlockSpec((1, padded, chunk), lambda c, *_: (item, 0, jnp.minimum(c, half_steps - 1)))

    pre_mine_shape = (items, padded, hidden // 2 if direct else hidden)
    pre_theirs_shape = (items, padded, hidden // 2 if direct else chunk)

    def ffn(item, merged, blocks, prev):
        half_out = lambda p: Out((items, padded, width // 2), BF16, at_item(item, padded, width // 2), p)
        return call(
            functools.partial(ffn_kernel, parts, item, direct),
            "ffn",
            (chunks,),
            [seq_index],
            [
                (loss_weight, scalars()),
                (merged, whole((seg, width))),
                (out_grad, at_item(item, seg, width)),
                (proj_weight, whole((width, width))),
                (row(proj_bias), whole((1, width))),
                (row(ffn_norm_gain), whole((1, width))),
                (row(ffn_norm_bias), whole((1, width))),
                (up_weight, pl.BlockSpec((width, chunk), lambda c, seq: (0, chunk_of(c, seq)))),
                (row(up_bias), pl.BlockSpec((1, chunk), lambda c, seq: (0, chunk_of(c, seq)))),
                (down_weight, pl.BlockSpec((chunk, width), lambda c, seq: (chunk_of(c, seq), 0))),
                (row(down_bias), whole((1, width))),
            ]
            + [(block, whole((seg, local))) for block in blocks],
            [Out((seg, local), BF16, whole((seg, local))) for _ in range(parts)]
            + [
                Out((items, seg, width), BF16, at_item(item, seg, width), prev[0]),
                Out((seg, width), F32, whole((seg, width))),
                Out((items, padded, width), BF16, at_item(item, padded, width), prev[1]),
                Out((items, padded, width), BF16, at_item(item, padded, width), prev[2]),
                Out(
                    (items, padded, hidden),
                    BF16,
                    pl.BlockSpec((1, padded, chunk), lambda c, seq: (item, 0, chunk_of(c, seq))),
                    prev[3],
                ),
                Out(pre_mine_shape, BF16, pre_spec(item, True), prev[4]),
                Out(pre_theirs_shape, BF16, pre_spec(item, False), prev[5]),
                half_out(prev[6]),
                half_out(prev[7]),
                half_out(prev[8]),
                half_out(prev[9]),
                Out((1, hidden), F32, pl.BlockSpec((1, chunk), lambda c, seq: (0, chunk_of(c, seq)))),
                Out((4, width), F32, whole((4, width))),
            ],
            [
                vmem((seg, width), F32),
                vmem((seg, width), BF16),
                vmem((seg, width), BF16),
                vmem((seg, width), F32),
                vmem((seg, width), F32),
                vmem((seg, width), BF16),
                vmem((parts, seg, local), BF16),
                vmem((2, padded, width // 2), BF16),
            ],
            2 * seg * width * (4 * hidden + 2 * width),
            4 * width * hidden + 2 * width * width + 4 * seg * hidden + 24 * seg * width,
        )

    def tail(item, merged, d_after, blocks, prev, after):
        return call(
            functools.partial(tail_kernel, parts),
            "tail",
            (3,),
            [seq_index],
            [
                (merged, whole((seg, width))),
                (d_after, whole((seg, width))),
                (row(attn_norm_gain), whole((1, width))),
                (qkv_weight, pl.BlockSpec((width, width), lambda c, *_: (0, c))),
            ]
            + [(block, whole((seg, 3 * local))) for block in blocks],
            [
                Out((items, seg, width), BF16, at_item(item, seg, width), prev[0]),
                Out((items, padded, 3 * width // 2), BF16, at_item(item, padded, 3 * width // 2), prev[1]),
                Out((items, padded, 3 * width // 2), BF16, at_item(item, padded, 3 * width // 2), prev[2]),
                Out((items, padded, width // 2), BF16, at_item(item, padded, width // 2), prev[3]),
                Out((items, padded, width // 2), BF16, at_item(item, padded, width // 2), prev[4]),
                Out((4, width), F32, whole((4, width))),
            ],
            [
                vmem((seg, width), F32),
                vmem((3, seg, width), BF16),
                vmem((parts, seg, 3 * local), BF16),
                vmem((2, padded, width // 2), BF16),
                vmem((2, padded, 3 * width // 2), BF16),
                vmem((seg, 3 * width), BF16),
            ],
            2 * seg * width * width * 3,
            6 * width * width + 26 * seg * width,
            after,
        )

    def input_grads(d_merged, after):
        one = lambda pick: pl.BlockSpec((1, seg, width), pick)
        return call(
            input_grads_kernel,
            "input_grads",
            (2, items),
            [],
            [
                (d_merged, one(lambda h, i: (i, 0, 0))),
                (skip_weight, pl.BlockSpec((width, width), lambda h, i: (h, 0))),
            ],
            [
                Out((items, seg, width), BF16, one(lambda h, i: (jnp.where(h == 0, i, items - 1), 0, 0))),
                Out((items, seg, width), BF16, one(lambda h, i: (jnp.where(h == 0, 0, i), 0, 0))),
            ],
            [],
            4 * items * seg * width * width,
            4 * width * width + 6 * items * seg * width,
            after,
        )

    flat = lambda v: v.reshape(items * padded, v.shape[-1])

    kept, merged_rows = [None, None], []
    head_blocks, sent = [], []
    for item in range(items):
        *blocks, merged, normed, cat = front(item, kept)
        kept = [normed, cat]
        merged_rows.append(merged)
        head_blocks.append(exchange(blocks))
    normed_attn, both_tokens = kept

    returned, log_sums = [], []
    for item in range(items):
        *outs, log_sum = attend(item, head_blocks[item])
        log_sums.append(log_sum)
        returned.append(exchange(outs))

    kept = [None] * 10
    d_heads, d_afters, up_bias_rows, vector_rows = [], [], [], []
    for item in range(items):
        results = ffn(item, merged_rows[item], returned[item], kept)
        d_heads.append(exchange(results[:parts]))
        rest = results[parts:]
        kept = [rest[0], *rest[2:11]]
        d_afters.append(rest[1])
        up_bias_rows.append(rest[11])
        vector_rows.append(rest[12])
    block_out, normed_ffn, attended, activ, pre_mine, pre_theirs, down_mine, down_theirs, branch_mine, branch_theirs = kept
    if direct:
        pre_mine, pre_theirs = flat(pre_mine), flat(pre_theirs)
    else:
        even, odd = (parity_blocks(flat(pre_mine), hidden // parts, p) for p in range(2))
        pre_mine, pre_theirs = (jnp.where(me % 2 == p, even, odd) for p in range(2))
    core, x = ("seq", 1), ("seq", 2)
    y, z_near, z_far = ("dp", 1), ("dp", 2), ("dp", 4)
    down = ScatterSum(flat(activ), flat(down_theirs))
    up = ScatterSum(flat(normed_ffn), tie(pre_theirs, down.sent))
    down.join(tie(flat(down_mine), up.sent), (1, [y, z_near, z_far, x]))
    up.join(tie(pre_mine, down.flows[0].send), (1, [z_near, x, y, z_far]))

    d_packed = []
    for item in range(items):
        after = []
        if item == 0:
            after = [down.flows[0].send, up.flows[0].send]
        if item == items - 1:
            after = down.advance() + up.advance()
        d_packed.append(
            exchange(attend_back(item, head_blocks[item], d_heads[item], log_sums[item], after))
        )

    kept = [None] * 5
    tail_rows = []
    for item in range(items):
        after = down.advance() + up.advance() if item == 1 else []
        *kept, vectors = tail(item, merged_rows[item], d_afters[item], d_packed[item], kept, after)
        tail_rows.append(vectors)
    d_merged, pack_mine, pack_theirs, merge_mine, merge_theirs = kept

    vectors = jnp.concatenate([sum(tail_rows), sum(vector_rows), sum(up_bias_rows).reshape(-1, width)], axis=0)
    steps = [*axis_bits("seq", 2), *reversed(axis_bits("dp")), core]

    def spread(value, *after):
        return value + xor_permute(tie(value, *after), *steps.pop(0)) if steps else value

    qkv = ScatterSum(flat(normed_attn), flat(pack_theirs))
    vectors = spread(vectors)
    skip = ScatterSum(flat(both_tokens), tie(flat(merge_theirs), vectors, qkv.sent))
    vectors = spread(vectors, skip.sent)
    sent = qkv.join(tie(flat(pack_mine), skip.sent), (0.56, [x, y, z_near, z_far]), (0.44, [z_near, y, z_far, x]))
    vectors = spread(vectors, *sent)
    sent = skip.join(tie(flat(merge_mine), *sent), (1, [y, z_near, z_far, x]))
    vectors = spread(vectors, *sent)
    tokens_grad, skip_grad = input_grads(d_merged, sent)
    proj = ScatterSum(flat(attended), tie(flat(branch_theirs), tokens_grad))
    sent = proj.join(flat(branch_mine), (1, [y, z_near, z_far, x]))
    while steps:
        vectors = spread(vectors)
    qkv.advance(*sent)
    late, early = vectors[:4], vectors[4:]
    final_down, final_up = down.finish(), up.finish()
    final_qkv, final_skip, final_proj = qkv.finish(), skip.finish(), proj.finish()
    return (
        block_out,
        tokens_grad,
        skip_grad,
        final_skip,
        final_qkv,
        final_proj,
        final_up,
        final_down,
        late[2],
        late[0],
        late[1],
        early[3],
        early[1],
        early[2],
        early[4:].reshape(-1),
        early[0],
    )


def solution(mesh):
    rows = P("dp", "seq", None)
    in_specs = (rows, rows) + (P(),) * 13 + (P("dp", None), P("dp"), rows)
    out_specs = (rows,) * 3 + (P("dp", "seq"),) * 5 + (P(),) * 8
    return jax.shard_map(body, mesh=mesh, in_specs=in_specs, out_specs=out_specs, check_vma=False)
```
